32 devices in a mesh: blk: 4 (over y, x), sta: 8 (over z, core).
Axes of the slice: x: 2, y: 2, z: 4, core: 2. Of those that a mesh axis runs over, the one named last changes fastest.
Arguments:
- waveforms: bfloat16 [48, 2048], P('sta', 'blk')
- templates: bfloat16 [48, 409600], P('sta', 'blk')
- available: int32 [16, 1024], P(None, 'blk'), may hold values from 0 to 1, as said below
- usable: int32 [48], replicated, may hold values from 0 to 1
Outputs:
- detection: float32 [1024, 2048], P(('blk', 'sta'))
The draws below stay inside these ranges and needn't reach their ends.
Inputs may be any that keep to these rules, and one draw needn't show every extreme that they name: Each template is available on one run of consecutive stations and nowhere else.
All inputs are finite; a program needn't handle non-finite values.
Results may differ from the reference program's by a relative error of at most 0.003.
Values may be sent and summed in bfloat16 or wider, within the bound.
No kernel may reach another device: no remote copies, remote signals or barrier semaphores. Data moves between devices by JAX's collectives and lax.ppermute only.
A program may use at most 128 MiB of HBM per device.

```python
import jax
import jax.numpy as jnp
from jax import lax

TLEN = 400
TEMPLATES = 1024
STATIONS = 16
CHANNELS = 48
NLAG = 2048


def draw_waveforms(key, part):
    first_key, second_key, third_key = jax.random.split(key, 3)
    noise = jax.random.normal(first_key, (CHANNELS, NLAG), jnp.float32)
    level = jnp.exp(jax.random.uniform(second_key, (CHANNELS, 1, 1), jnp.float32, 0.0, 2.3))
    envelope = jnp.exp(jax.random.uniform(third_key, (CHANNELS, NLAG // 32, 1), jnp.float32, -0.69, 0.69))
    shaped = noise.reshape(CHANNELS, NLAG // 32, 32) * level * envelope
    return shaped.reshape(CHANNELS, NLAG).astype(jnp.bfloat16)


def draw_templates(key, part):
    first_key, second_key, third_key = jax.random.split(key, 3)
    noise = jax.random.normal(first_key, (CHANNELS, TEMPLATES, TLEN), jnp.float32)
    spread = jnp.exp(jax.random.uniform(second_key, (CHANNELS, TEMPLATES, 1), jnp.float32, 0.0, 2.3))
    offset = jax.random.uniform(third_key, (CHANNELS, TEMPLATES, 1), jnp.float32, -1.0, 1.0)
    return ((noise + offset) * spread).reshape(CHANNELS, TEMPLATES * TLEN).astype(jnp.bfloat16)


def draw_available(key, part):
    first_key, second_key = jax.random.split(key, 2)
    centre = jax.random.randint(first_key, (1, TEMPLATES), 0, STATIONS)
    radius = jax.random.randint(second_key, (1, TEMPLATES), 0, max(STATIONS // 4, 2))
    station_ids = jnp.arange(STATIONS, dtype=jnp.int32)[:, None]
    return (jnp.abs(station_ids - centre) <= radius).astype(jnp.int32)


def draw_usable(key, part):
    first_key, second_key = jax.random.split(key, 2)
    station_alive = jax.random.randint(first_key, (STATIONS, 1), 0, 4) > 0
    component_alive = jax.random.randint(second_key, (STATIONS, 3), 0, 8) > 0
    return jnp.logical_and(station_alive, component_alive).reshape(CHANNELS).astype(jnp.int32)


def setup_inputs(seed: int = 0) -> dict:
    seeds = jax.random.split(jax.random.key(seed), 5)
    waveforms = draw_waveforms(jax.random.fold_in(seeds[4], 71), 0)
    templates = draw_templates(jax.random.fold_in(seeds[4], 71), 0)
    available = draw_available(jax.random.fold_in(seeds[4], 71), 0)
    usable = draw_usable(jax.random.fold_in(seeds[4], 71), 0)
    return dict(waveforms=waveforms, templates=templates, available=available, usable=usable)


def correlate(signal, kernels):
    groups, per_group, length = kernels.shape
    stacked = kernels.reshape(groups * per_group, 1, length)
    result = lax.conv_general_dilated(signal[None], stacked, (1,), 'VALID', dimension_numbers=('NCH', 'OIH', 'NCH'), feature_group_count=groups, precision=lax.Precision.HIGHEST, preferred_element_type=jnp.float32)
    return result[0].reshape(groups, per_group, result.shape[2])

def reference(waveforms, templates, available, usable):
    padded = jnp.pad(waveforms, ((0, 0), (0, TLEN - 1)))
    squares = padded.astype(jnp.float32) ** 2
    running = jnp.concatenate([jnp.zeros((CHANNELS, 1), jnp.float32), jnp.cumsum(squares, axis=1)], axis=1)
    energy = running[:, TLEN:] - running[:, :NLAG]
    scale = 1.0 / jnp.sqrt(jnp.maximum(energy, 0.1 * TLEN))
    weight = jnp.repeat(available, 3, axis=0).astype(jnp.float32) * usable.astype(jnp.float32)[:, None]

    def one_station(summed, station):
        first_row = (station * 3).astype(jnp.int32)
        raw = lax.dynamic_slice_in_dim(templates, first_row, 3, 0).astype(jnp.float32).reshape(3, TEMPLATES, TLEN)
        centred = raw - lax.optimization_barrier(jnp.mean(raw, axis=2, keepdims=True))
        norms = jnp.sqrt(lax.optimization_barrier(jnp.sum(centred * centred, axis=2, keepdims=True)) + 1e-06)
        factor = lax.dynamic_slice_in_dim(weight, first_row, 3, 0)
        rounded = (centred / norms * factor[:, :, None]).astype(jnp.bfloat16)
        rounded = lax.optimization_barrier(rounded)
        kernels = rounded.astype(jnp.float32)
        signal = lax.dynamic_slice_in_dim(padded, first_row, 3, 0).astype(jnp.float32)
        matched = correlate(signal, kernels)
        rows_scale = lax.dynamic_slice_in_dim(scale, first_row, 3, 0)
        return (summed + lax.optimization_barrier(jnp.sum(matched * rows_scale[:, None, :], axis=0)), None)
    stack_sum, unused = lax.scan(one_station, jnp.zeros((TEMPLATES, NLAG), jnp.float32), jnp.arange(STATIONS, dtype=jnp.int32))
    station_usable = lax.optimization_barrier(jnp.sum(usable.reshape(STATIONS, 3), axis=1)).astype(jnp.float32)
    counted = lax.optimization_barrier(jnp.sum(available.astype(jnp.float32) * station_usable[:, None], axis=0))
    return jnp.sqrt(jnp.float32(TLEN)) * stack_sum / jnp.sqrt(jnp.maximum(counted, 1.0))[:, None]
```

```python
import functools
import math

import jax
import jax.numpy as jnp
from jax import lax
from jax.experimental import pallas as pl
from jax.experimental.pallas import tpu as pltpu
from jax.sharding import PartitionSpec as P

TLEN = 400
COMPONENTS = 3
LANES = 128
SUBLANES = 8

FLOOR_SHARE = 0.1
EPSILON = 1e-06

PERIOD = LANES // math.gcd(TLEN, LANES)
PERIOD_TILES = PERIOD * TLEN // LANES
DEPTH_TILES = -(-TLEN // LANES)
DEPTH = DEPTH_TILES * LANES
VMEM_LIMIT = 48 << 20


def exchanged(array, axis, by):
    length = lax.axis_size(axis)
    return lax.ppermute(array, axis, [(i, i ^ by) for i in range(length)])


def template_kernel(shares, raw_ref, avail_ref, usable_ref, out_ref, flat, rows, avail_cols):
    channels, width = raw_ref.shape
    stations, count = avail_ref.shape
    groups = count // PERIOD
    tiles = width // LANES
    stations_here = channels // COMPONENTS
    own = count // shares
    me = lax.axis_index("sta")

    unroll = 8 if tiles % 8 == 0 else 1

    def spread(step, carry):
        for sub in range(unroll):
            tile = step * unroll + sub
            piece = raw_ref[:, pl.ds(pl.multiple_of(tile * LANES, LANES), LANES)]
            flat[pl.ds(pl.multiple_of(tile * SUBLANES, SUBLANES), channels), :] = piece.astype(
                jnp.float32
            )
        return carry

    lax.fori_loop(0, tiles // unroll, spread, 0)

    station_row = lax.broadcasted_iota(jnp.int32, (stations, LANES), 0)
    avail = avail_ref[...].astype(jnp.float32)
    for local_station in range(stations_here):
        chosen = (station_row == me * stations_here + local_station).astype(jnp.float32)
        avail_cols[local_station] = lax.dot_general(
            avail, chosen, (((0,), (0,)), ((), ())), preferred_element_type=jnp.float32
        )

    lane = lax.broadcasted_iota(jnp.int32, (groups, LANES), 1)
    last = TLEN - (DEPTH_TILES - 1) * LANES
    block_lane = lax.broadcasted_iota(jnp.int32, (own, LANES), 1)

    def one_channel(channel, carry):
        for which in range(PERIOD):
            first, offset = divmod(which * TLEN, LANES)
            pieces = []
            for part in range(DEPTH_TILES):
                start = (first + part) * SUBLANES + channel
                piece = flat[pl.ds(start, groups, stride=PERIOD_TILES * SUBLANES), :]
                if offset:
                    piece = pltpu.roll(piece, LANES - offset, 1)
                pieces.append(piece)
            for part in range(DEPTH_TILES):
                value = pieces[part]
                if part + 1 < DEPTH_TILES:
                    if offset:
                        value = jnp.where(lane < LANES - offset, value, pieces[part + 1])
                else:
                    value = jnp.where(lane < last, value, 0.0)
                rows[part, pl.ds(which, groups, stride=PERIOD), :] = value
        use = usable_ref[me * channels + channel].astype(jnp.float32)
        for place in range(shares):
            core, chip = divmod(place, shares // 2)
            owner = me ^ (chip * 2 + core)
            here = pl.ds(pl.multiple_of(owner * own, own), own)
            parts = [rows[part, here, :] for part in range(DEPTH_TILES)]
            mean = jnp.sum(sum(parts), axis=1, keepdims=True) * (1.0 / TLEN)
            centred = [value - mean for value in parts]
            centred[-1] = jnp.where(block_lane < last, centred[-1], 0.0)
            squared = jnp.sum(sum(value * value for value in centred), axis=1, keepdims=True)
            weight = avail_cols[channel // COMPONENTS, here, :] * use
            factor = lax.rsqrt(squared + EPSILON) * weight
            for part in range(DEPTH_TILES):
                out_ref[
                    channel, place * own : (place + 1) * own, part * LANES : (part + 1) * LANES
                ] = (centred[part] * factor).astype(jnp.bfloat16)
        return carry

    lax.fori_loop(0, channels, one_channel, 0)


def weighted_templates(raw, available, usable, shares):
    channels, width = raw.shape
    stations, count = available.shape
    return pl.pallas_call(
        functools.partial(template_kernel, shares),
        out_shape=jax.ShapeDtypeStruct((channels, count, DEPTH), jnp.bfloat16),
        in_specs=[
            pl.BlockSpec(memory_space=pltpu.VMEM),
            pl.BlockSpec(memory_space=pltpu.VMEM),
            pl.BlockSpec(memory_space=pltpu.SMEM),
        ],
        out_specs=pl.BlockSpec(memory_space=pltpu.VMEM),
        scratch_shapes=[
            pltpu.VMEM((width // LANES * SUBLANES, LANES), jnp.float32),
            pltpu.VMEM((DEPTH_TILES, count, LANES), jnp.float32),
            pltpu.VMEM((channels // COMPONENTS, count, LANES), jnp.float32),
        ],
        compiler_params=pltpu.CompilerParams(vmem_limit_bytes=VMEM_LIMIT),
        cost_estimate=pl.CostEstimate(
            flops=20 * channels * count * DEPTH, transcendentals=0, bytes_accessed=4 << 20
        ),
        name="templates",
    )(raw, available, usable)


def correlate_kernel(blocks, weighted_ref, *refs):
    segments = refs[:blocks]
    mine_ref, other_ref, record, windows, scale = refs[blocks:]
    channels, count, depth = weighted_ref.shape
    segment = segments[0].shape[1]
    lags = blocks * segment
    wide = record.shape[1]
    base = windows.shape[2]
    half = count // 2
    me = lax.axis_index("blk")

    record[...] = jnp.zeros_like(record)
    for by in range(blocks):
        start = pl.multiple_of((me ^ by) * segment, LANES)
        record[0:channels, pl.ds(start, segment)] = segments[by][...].astype(jnp.float32)

    def ahead(value, by):
        return pltpu.roll(value, value.shape[1] - by, 1) if by else value

    samples = record[...]
    power = samples * samples
    energy, taken, span = None, 0, 1
    while True:
        if TLEN & span:
            term = ahead(power, taken)
            energy = term if energy is None else energy + term
            taken += span
        if 2 * span > TLEN:
            break
        power = power + ahead(power, span)
        span *= 2
    scale[...] = lax.rsqrt(jnp.maximum(energy[:, :lags], FLOOR_SHARE * TLEN))

    sublane = lax.broadcasted_iota(jnp.int32, (SUBLANES, wide), 0)
    for channel in range(channels):
        shifted = jnp.broadcast_to(record[channel : channel + 1, :], (SUBLANES, wide))
        for bit in (1, 2, 4):
            shifted = jnp.where((sublane & bit) != 0, ahead(shifted, bit), shifted)
        for row in range(0, LANES, 2 * SUBLANES):
            pair = jnp.concatenate(
                [
                    ahead(shifted, row)[:, :base],
                    ahead(shifted, row + SUBLANES)[:, :base],
                ],
                axis=0,
            )
            windows[channel, row : row + 2 * SUBLANES, :] = pair.astype(jnp.bfloat16)

    tile = 2 * LANES

    def one_tile(step, carry):
        first = step * tile
        total = None
        for channel in range(channels):
            signal = jnp.concatenate(
                [
                    windows[channel, :, pl.ds(pl.multiple_of(first + part * LANES, LANES), tile)]
                    for part in range(depth // LANES)
                ],
                axis=0,
            )
            matched = jnp.dot(weighted_ref[channel], signal, preferred_element_type=jnp.float32)
            here = pl.ds(pl.multiple_of(first, LANES), tile)
            term = matched * scale[channel : channel + 1, here]
            total = term if total is None else total + term
        here = pl.ds(pl.multiple_of(first, LANES), tile)
        mine_ref[:, here] = total[:half]
        other_ref[:, here] = total[half:].astype(other_ref.dtype)
        return carry

    lax.fori_loop(0, lags // tile, one_tile, 0)


def correlations(weighted, segments):
    channels, count, depth = weighted.shape
    blocks = len(segments)
    lags = blocks * segments[0].shape[1]
    half = count // 2
    return pl.pallas_call(
        functools.partial(correlate_kernel, blocks),
        out_shape=(
            jax.ShapeDtypeStruct((half, lags), jnp.float32),
            jax.ShapeDtypeStruct((half, lags), jnp.bfloat16),
        ),
        in_specs=[pl.BlockSpec(memory_space=pltpu.VMEM)] * (1 + blocks),
        out_specs=(pl.BlockSpec(memory_space=pltpu.VMEM),) * 2,
        scratch_shapes=[
            pltpu.VMEM((SUBLANES, lags + depth + LANES), jnp.float32),
            pltpu.VMEM((channels, LANES, lags + depth), jnp.bfloat16),
            pltpu.VMEM((SUBLANES, lags), jnp.float32),
        ],
        compiler_params=pltpu.CompilerParams(vmem_limit_bytes=VMEM_LIMIT),
        cost_estimate=pl.CostEstimate(
            flops=2 * channels * count * depth * lags, transcendentals=0, bytes_accessed=4 << 20
        ),
        name="correlate",
    )(weighted, *segments)


def local(waveforms, templates, available, usable):
    blocks = lax.axis_size("blk")
    shares = lax.axis_size("sta")
    my_share = lax.axis_index("sta")
    block_rows = available.shape[1]
    own_rows = block_rows // shares
    chips = shares // 2

    segments = {0: waveforms}
    for by in reversed(range(1, blocks)):
        segments[by] = exchanged(waveforms, "blk", by)
    weighted = weighted_templates(templates, available, usable, shares)
    mine, other = correlations(weighted, [segments[by] for by in range(blocks)])
    summed = mine + exchanged(other, "sta", 1).astype(jnp.float32)
    summed = summed.reshape(chips, own_rows, summed.shape[1])
    order = sorted(range(1, chips), key=lambda by: -(by ^ (by >> 1)))
    arrived = [
        exchanged(summed[by].astype(jnp.bfloat16), "sta", 2 * by) for by in order
    ]
    stacked = summed[0]
    for term in arrived:
        stacked = stacked + term.astype(jnp.float32)

    station_usable = jnp.sum(usable.reshape(-1, COMPONENTS), axis=1).astype(jnp.float32)
    owned = lax.dynamic_slice_in_dim(available, my_share * own_rows, own_rows, 1)
    counted = jnp.sum(owned.astype(jnp.float32) * station_usable[:, None], axis=0)
    return math.sqrt(TLEN) * stacked * lax.rsqrt(jnp.maximum(counted, 1.0))[:, None]


def solution(mesh):
    return jax.shard_map(
        local,
        mesh=mesh,
        in_specs=(P("sta", "blk"), P("sta", "blk"), P(None, "blk"), P()),
        out_specs=P(("blk", "sta"), None),
        check_vma=False,
    )
```

```python
import functools
import math

import jax
import jax.numpy as jnp
from jax import lax
from jax.experimental import pallas as pl
from jax.experimental.pallas import tpu as pltpu
from jax.sharding import PartitionSpec as P

TLEN = 400
COMPONENTS = 3
LANES = 128
SUBLANES = 8

FLOOR_SHARE = 0.1
EPSILON = 1e-06

PERIOD = LANES // math.gcd(TLEN, LANES)
PERIOD_TILES = PERIOD * TLEN // LANES
DEPTH_TILES = -(-TLEN // LANES)
DEPTH = DEPTH_TILES * LANES
VMEM_LIMIT = 24 << 20


def exchanged(array, axis, by):
    length = lax.axis_size(axis)
    return lax.ppermute(array, axis, [(i, i ^ by) for i in range(length)])


def template_kernel(
    shares, raw_ref, avail_ref, usable_ref, out_ref, flat, rows, avail_cols
):
    channels, width = raw_ref.shape
    stations, count = avail_ref.shape
    groups = count // PERIOD
    tiles = width // LANES
    stations_here = channels // COMPONENTS
    own = count // shares
    me = lax.axis_index("sta")
    unroll = next(by for by in (16, 10, 8, 5, 4, 2, 1) if tiles % by == 0)

    def spread(step, carry):
        for sub in range(unroll):
            tile = step * unroll + sub
            value = raw_ref[:, pl.ds(pl.multiple_of(tile * LANES, LANES), LANES)]
            flat[pl.ds(pl.multiple_of(tile * SUBLANES, SUBLANES), channels), :] = value.astype(
                jnp.float32
            )
        return carry

    lax.fori_loop(0, tiles // unroll, spread, 0)

    station_row = lax.broadcasted_iota(jnp.int32, (stations, LANES), 0)
    avail = avail_ref[...].astype(jnp.float32)
    for local_station in range(stations_here):
        chosen = (station_row == me * stations_here + local_station).astype(jnp.float32)
        avail_cols[local_station] = lax.dot_general(
            avail, chosen, (((0,), (0,)), ((), ())), preferred_element_type=jnp.float32
        )

    lane = lax.broadcasted_iota(jnp.int32, (groups, LANES), 1)
    last = TLEN - (DEPTH_TILES - 1) * LANES
    block_lane = lax.broadcasted_iota(jnp.int32, (own, LANES), 1)

    def one_channel(channel, carry):
        for which in range(PERIOD):
            first, offset = divmod(which * TLEN, LANES)
            pieces = []
            for part in range(DEPTH_TILES):
                start = (first + part) * SUBLANES + channel
                piece = flat[pl.ds(start, groups, stride=PERIOD_TILES * SUBLANES), :]
                if offset:
                    piece = pltpu.roll(piece, LANES - offset, 1)
                pieces.append(piece)
            for part in range(DEPTH_TILES):
                value = pieces[part]
                if part + 1 < DEPTH_TILES:
                    if offset:
                        value = jnp.where(lane < LANES - offset, value, pieces[part + 1])
                else:
                    value = jnp.where(lane < last, value, 0.0)
                rows[part, pl.ds(which, groups, stride=PERIOD), :] = value
        use = usable_ref[me * channels + channel].astype(jnp.float32)
        for place in range(shares):
            core, chip = divmod(place, shares // 2)
            owner = me ^ (chip * 2 + core)
            here = pl.ds(pl.multiple_of(owner * own, own), own)
            parts = [rows[part, here, :] for part in range(DEPTH_TILES)]
            mean = jnp.sum(sum(parts), axis=1, keepdims=True) * (1.0 / TLEN)
            centred = [value - mean for value in parts]
            centred[-1] = jnp.where(block_lane < last, centred[-1], 0.0)
            squared = jnp.sum(sum(value * value for value in centred), axis=1, keepdims=True)
            weight = avail_cols[channel // COMPONENTS, here, :] * use
            factor = lax.rsqrt(squared + EPSILON) * weight
            for part in range(DEPTH_TILES):
                out_ref[
                    channel, place * own : (place + 1) * own, part * LANES : (part + 1) * LANES
                ] = (centred[part] * factor).astype(jnp.bfloat16)
        return carry

    lax.fori_loop(0, channels, one_channel, 0)


def weighted_templates(raw, available, usable, shares):
    channels, width = raw.shape
    stations, count = available.shape
    return pl.pallas_call(
        functools.partial(template_kernel, shares),
        out_shape=jax.ShapeDtypeStruct((channels, count, DEPTH), jnp.bfloat16),
        in_specs=[
            pl.BlockSpec(memory_space=pltpu.VMEM),
            pl.BlockSpec(memory_space=pltpu.VMEM),
            pl.BlockSpec(memory_space=pltpu.SMEM),
        ],
        out_specs=pl.BlockSpec(memory_space=pltpu.VMEM),
        scratch_shapes=[
            pltpu.VMEM((width // LANES * SUBLANES, LANES), jnp.float32),
            pltpu.VMEM((DEPTH_TILES, count, LANES), jnp.float32),
            pltpu.VMEM((channels // COMPONENTS, count, LANES), jnp.float32),
        ],
        compiler_params=pltpu.CompilerParams(vmem_limit_bytes=VMEM_LIMIT),
        cost_estimate=pl.CostEstimate(flops=1 << 10, transcendentals=0, bytes_accessed=1 << 10),
        name="templates",
    )(raw, available, usable)


def ahead(value, by):
    return pltpu.roll(value, value.shape[1] - by, 1) if by else value


def correlate_kernel(blocks, weighted_ref, *refs):
    segments = refs[:blocks]
    mine_ref, other_ref, scale, record, windows = refs[blocks:]
    channels, segment = segments[0].shape
    lags = blocks * segment
    wide = record.shape[1]
    base = windows.shape[2]
    me = lax.axis_index("blk")

    record[:, lags:] = jnp.zeros((SUBLANES, wide - lags), jnp.float32)
    for by in range(blocks):
        start = pl.multiple_of((me ^ by) * segment, LANES)
        record[0:channels, pl.ds(start, segment)] = segments[by][...].astype(jnp.float32)

    power = record[...] * record[...]
    energy, taken, span = None, 0, 1
    while True:
        if TLEN & span:
            term = ahead(power, taken)
            energy = term if energy is None else energy + term
            taken += span
        if 2 * span > TLEN:
            break
        power = power + ahead(power, span)
        span *= 2
    scale[...] = lax.rsqrt(jnp.maximum(energy[:, :lags], FLOOR_SHARE * TLEN))

    sublane = lax.broadcasted_iota(jnp.int32, (SUBLANES, wide), 0)
    for channel in range(channels):
        shifted = jnp.broadcast_to(record[channel : channel + 1, :], (SUBLANES, wide))
        for bit in (1, 2, 4):
            shifted = jnp.where((sublane & bit) != 0, ahead(shifted, bit), shifted)
        pair = jnp.concatenate([shifted, ahead(shifted, SUBLANES)], axis=0).astype(jnp.bfloat16)
        for row in range(0, LANES, 2 * SUBLANES):
            windows[channel, row : row + 2 * SUBLANES, :] = ahead(pair, row)[:, :base]

    half = weighted_ref.shape[1] // 2
    depth = weighted_ref.shape[2]
    tile = next(by for by in (8 * LANES, 4 * LANES, 2 * LANES, LANES) if lags % by == 0)

    def one_tile(step, carry):
        first = step * tile
        here = pl.ds(pl.multiple_of(first, LANES), tile)
        total = None
        for channel in range(channels):
            signal = jnp.concatenate(
                [
                    windows[channel, :, pl.ds(pl.multiple_of(first + part * LANES, LANES), tile)]
                    for part in range(depth // LANES)
                ],
                axis=0,
            )
            matched = jnp.dot(weighted_ref[channel], signal, preferred_element_type=jnp.float32)
            term = matched * scale[channel : channel + 1, here]
            total = term if total is None else total + term
        mine_ref[:, here] = total[:half]
        other_ref[:, here] = total[half:].astype(other_ref.dtype)
        return carry

    lax.fori_loop(0, lags // tile, one_tile, 0)


def correlations(weighted, segments):
    channels, count, depth = weighted.shape
    segment = segments[0].shape[1]
    blocks = len(segments)
    lags = blocks * segment
    return pl.pallas_call(
        functools.partial(correlate_kernel, blocks),
        out_shape=(
            jax.ShapeDtypeStruct((count // 2, lags), jnp.float32),
            jax.ShapeDtypeStruct((count // 2, lags), jnp.bfloat16),
        ),
        in_specs=[pl.BlockSpec(memory_space=pltpu.VMEM)] * (1 + blocks),
        out_specs=(pl.BlockSpec(memory_space=pltpu.VMEM),) * 2,
        scratch_shapes=[
            pltpu.VMEM((SUBLANES, lags), jnp.float32),
            pltpu.VMEM((SUBLANES, lags + depth), jnp.float32),
            pltpu.VMEM((channels, LANES, lags + depth - LANES), jnp.bfloat16),
        ],
        compiler_params=pltpu.CompilerParams(vmem_limit_bytes=VMEM_LIMIT),
        cost_estimate=pl.CostEstimate(flops=1 << 10, transcendentals=0, bytes_accessed=1 << 10),
        name="correlate",
    )(weighted, *segments)


def first_kernel(waveforms_ref, out_ref):
    out_ref[...] = waveforms_ref[...]


def first(waveforms):
    return pl.pallas_call(
        first_kernel,
        out_shape=jax.ShapeDtypeStruct(waveforms.shape, waveforms.dtype),
        in_specs=[pl.BlockSpec(memory_space=pltpu.VMEM)],
        out_specs=pl.BlockSpec(memory_space=pltpu.VMEM),
        cost_estimate=pl.CostEstimate(flops=1 << 36, transcendentals=0, bytes_accessed=1 << 26),
        compiler_params=pltpu.CompilerParams(vmem_limit_bytes=1 << 20),
        name="first",
    )(waveforms)


def local(waveforms, templates, available, usable):
    blocks = lax.axis_size("blk")
    shares = lax.axis_size("sta")
    my_share = lax.axis_index("sta")
    own_rows = available.shape[1] // shares
    chips = shares // 2

    waveforms = first(waveforms)
    segments = {0: waveforms}
    for by in reversed(range(1, blocks)):
        segments[by] = exchanged(waveforms, "blk", by)
    weighted = weighted_templates(templates, available, usable, shares)

    wide, narrow = jnp.float32, jnp.bfloat16
    mine, other = correlations(weighted, [segments[by] for by in range(blocks)])
    summed = (mine + exchanged(other, "sta", 1).astype(wide)).reshape(chips, own_rows, -1)
    stacked = summed[0]
    for by in sorted(range(1, chips), key=lambda by: -(by ^ (by >> 1))):
        term = exchanged(summed[by].astype(narrow), "sta", 2 * by)
        stacked = stacked + term.astype(wide)

    station_usable = jnp.sum(usable.reshape(-1, COMPONENTS), axis=1).astype(jnp.float32)
    owned = lax.dynamic_slice_in_dim(available, my_share * own_rows, own_rows, 1)
    counted = jnp.sum(owned.astype(jnp.float32) * station_usable[:, None], axis=0)
    return math.sqrt(TLEN) * stacked * lax.rsqrt(jnp.maximum(counted, 1.0))[:, None]


def solution(mesh):
    return jax.shard_map(
        local,
        mesh=mesh,
        in_specs=(P("sta", "blk"), P("sta", "blk"), P(None, "blk"), P()),
        out_specs=P(("blk", "sta"), None),
        check_vma=False,
    )
```

```python
import functools
import math

import jax
import jax.numpy as jnp
from jax import lax
from jax.experimental import pallas as pl
from jax.experimental.pallas import tpu as pltpu
from jax.sharding import PartitionSpec as P

TLEN = 400
COMPONENTS = 3
LANES = 128
SUBLANES = 8

FLOOR_SHARE = 0.1
EPSILON = 1e-06

PERIOD = LANES // math.gcd(TLEN, LANES)
PERIOD_TILES = PERIOD * TLEN // LANES
DEPTH_TILES = -(-TLEN // LANES)
DEPTH = DEPTH_TILES * LANES
VMEM_LIMIT = 24 << 20


def exchanged(array, axis, by):
    length = lax.axis_size(axis)
    return lax.ppermute(array, axis, [(i, i ^ by) for i in range(length)])


def template_kernel(
    shares, stay, raw_ref, avail_ref, usable_ref, token_ref, out_ref, flat, rows, avail_cols
):
    channels, width = raw_ref.shape
    stations, count = avail_ref.shape
    tiles = width // LANES
    stations_here = channels // COMPONENTS
    own = count // shares
    chips = shares // 2
    chip_rows = 2 * own
    chip_tiles = tiles // chips
    taken = range(1) if stay else range(1, chips)
    groups = len(taken) * chip_rows // PERIOD
    me = lax.axis_index("sta")
    start = me // 2 if stay else me // 2 + 1
    unroll = next(by for by in (25, 20, 16, 10, 8, 5, 4, 2, 1) if chip_tiles % by == 0)

    def spread(step, carry):
        source = lax.rem(start * chip_tiles + step * unroll, tiles)
        for sub in range(unroll):
            value = raw_ref[:, pl.ds(pl.multiple_of((source + sub) * LANES, LANES), LANES)]
            there = pl.multiple_of((step * unroll + sub) * SUBLANES, SUBLANES)
            flat[pl.ds(there, channels), :] = value.astype(jnp.float32)
        return carry

    lax.fori_loop(0, len(taken) * chip_tiles // unroll, spread, 0)

    station_row = lax.broadcasted_iota(jnp.int32, (stations, LANES), 0)
    avail = avail_ref[...].astype(jnp.float32)
    for local_station in range(stations_here):
        chosen = (station_row == me * stations_here + local_station).astype(jnp.float32)
        avail_cols[local_station] = lax.dot_general(
            avail, chosen, (((0,), (0,)), ((), ())), preferred_element_type=jnp.float32
        )

    lane = lax.broadcasted_iota(jnp.int32, (groups, LANES), 1)
    last = TLEN - (DEPTH_TILES - 1) * LANES
    block_lane = lax.broadcasted_iota(jnp.int32, (own, LANES), 1)

    def one_step(step, carry):
        channel = jnp.maximum(step - 1, 0)
        ready = 1 - step % 2
        use = usable_ref[me * channels + channel].astype(jnp.float32)
        for place in range(2 * len(taken)):
            core, chip = divmod(place, len(taken))
            owner = me ^ (2 * taken[chip] + core)
            moved = lax.rem(owner // 2 - start + chips, chips) * chip_rows + owner % 2 * own
            here = pl.ds(pl.multiple_of(moved, own), own)
            parts = [rows[ready, part, here, :] for part in range(DEPTH_TILES)]
            mean = jnp.sum(sum(parts), axis=1, keepdims=True) * (1.0 / TLEN)
            centred = [value - mean for value in parts]
            centred[-1] = jnp.where(block_lane < last, centred[-1], 0.0)
            squared = jnp.sum(sum(value * value for value in centred), axis=1, keepdims=True)
            there = pl.ds(pl.multiple_of(owner * own, own), own)
            weight = avail_cols[channel // COMPONENTS, there, :] * use
            factor = lax.rsqrt(squared + EPSILON) * weight
            for part in range(DEPTH_TILES):
                out_ref[
                    channel, place * own : (place + 1) * own, part * LANES : (part + 1) * LANES
                ] = (centred[part] * factor).astype(jnp.bfloat16)
        channel = jnp.minimum(step, channels - 1)
        filled = step % 2
        for which in range(PERIOD):
            first, offset = divmod(which * TLEN, LANES)
            pieces = []
            for part in range(DEPTH_TILES):
                begin = (first + part) * SUBLANES + channel
                piece = flat[pl.ds(begin, groups, stride=PERIOD_TILES * SUBLANES), :]
                if offset:
                    piece = pltpu.roll(piece, LANES - offset, 1)
                pieces.append(piece)
            for part in range(DEPTH_TILES):
                value = pieces[part]
                if part + 1 < DEPTH_TILES:
                    if offset:
                        value = jnp.where(lane < LANES - offset, value, pieces[part + 1])
                else:
                    value = jnp.where(lane < last, value, 0.0)
                rows[filled, part, pl.ds(which, groups, stride=PERIOD), :] = value
        return carry

    lax.fori_loop(0, channels + 1, one_step, 0)


def weighted_templates(raw, available, usable, token, shares, stay):
    channels, width = raw.shape
    stations, count = available.shape
    taken = 2 * count // shares if stay else count - 2 * count // shares
    return pl.pallas_call(
        functools.partial(template_kernel, shares, stay),
        out_shape=jax.ShapeDtypeStruct((channels, taken, DEPTH), jnp.bfloat16),
        in_specs=[
            pl.BlockSpec(memory_space=pltpu.VMEM),
            pl.BlockSpec(memory_space=pltpu.VMEM),
            pl.BlockSpec(memory_space=pltpu.SMEM),
            pl.BlockSpec(memory_space=pltpu.VMEM),
        ],
        out_specs=pl.BlockSpec(memory_space=pltpu.VMEM),
        scratch_shapes=[
            pltpu.VMEM((taken * TLEN // LANES * SUBLANES, LANES), jnp.float32),
            pltpu.VMEM((2, DEPTH_TILES, taken, LANES), jnp.float32),
            pltpu.VMEM((channels // COMPONENTS, count, LANES), jnp.float32),
        ],
        compiler_params=pltpu.CompilerParams(vmem_limit_bytes=VMEM_LIMIT),
        cost_estimate=pl.CostEstimate(flops=1 << 10, transcendentals=0, bytes_accessed=1 << 10),
        name="templates_staying" if stay else "templates_leaving",
    )(raw, available, usable, token)


def ahead(value, by):
    return pltpu.roll(value, value.shape[1] - by, 1) if by else value


def correlate_kernel(blocks, weighted_ref, *refs):
    segments = refs[:blocks]
    mine_ref, other_ref, scale, record, windows = refs[blocks:]
    channels, segment = segments[0].shape
    lags = blocks * segment
    wide = record.shape[1]
    base = windows.shape[2]
    me = lax.axis_index("blk")

    record[:, lags:] = jnp.zeros((SUBLANES, wide - lags), jnp.float32)
    for by in range(blocks):
        start = pl.multiple_of((me ^ by) * segment, LANES)
        record[0:channels, pl.ds(start, segment)] = segments[by][...].astype(jnp.float32)

    power = record[...] * record[...]
    energy, taken, span = None, 0, 1
    while True:
        if TLEN & span:
            term = ahead(power, taken)
            energy = term if energy is None else energy + term
            taken += span
        if 2 * span > TLEN:
            break
        power = power + ahead(power, span)
        span *= 2
    scale[...] = lax.rsqrt(jnp.maximum(energy[:, :lags], FLOOR_SHARE * TLEN))

    sublane = lax.broadcasted_iota(jnp.int32, (SUBLANES, wide), 0)

    def one_record(channel, carry):
        shifted = jnp.broadcast_to(record[pl.ds(channel, 1), :], (SUBLANES, wide))
        for bit in (1, 2, 4):
            shifted = jnp.where((sublane & bit) != 0, ahead(shifted, bit), shifted)
        pair = jnp.concatenate([shifted, ahead(shifted, SUBLANES)], axis=0).astype(jnp.bfloat16)
        for row in range(0, LANES, 2 * SUBLANES):
            windows[channel, row : row + 2 * SUBLANES, :] = pair[:, row : row + base]
        return carry

    lax.fori_loop(0, channels, one_record, 0, unroll=2)

    half = weighted_ref.shape[1] // 2
    tile = next(by * LANES for by in (16, 8, 4, 2, 1) if lags % (by * LANES) == 0)

    def one_tile(first):
        here = pl.ds(first, tile)
        total = None
        for channel in range(channels):
            signal = jnp.concatenate(
                [
                    windows[channel, : min(LANES, TLEN - start), pl.ds(first + start, tile)]
                    for start in range(0, TLEN, LANES)
                ],
                axis=0,
            )
            weights = weighted_ref[channel, :, :TLEN]
            matched = jnp.dot(weights, signal, preferred_element_type=jnp.float32)
            term = matched * scale[channel : channel + 1, here]
            total = term if total is None else total + term
        mine_ref[:, here] = total[:half]
        other_ref[:, here] = total[half:].astype(other_ref.dtype)

    for step in range(lags // tile):
        one_tile(step * tile)


def correlations(weighted, segments, name):
    channels, count, depth = weighted.shape
    segment = segments[0].shape[1]
    blocks = len(segments)
    lags = blocks * segment
    return pl.pallas_call(
        functools.partial(correlate_kernel, blocks),
        out_shape=(
            jax.ShapeDtypeStruct((count // 2, lags), jnp.float32),
            jax.ShapeDtypeStruct((count // 2, lags), jnp.bfloat16),
        ),
        in_specs=[pl.BlockSpec(memory_space=pltpu.VMEM)] * (1 + blocks),
        out_specs=(pl.BlockSpec(memory_space=pltpu.VMEM),) * 2,
        scratch_shapes=[
            pltpu.VMEM((SUBLANES, lags), jnp.float32),
            pltpu.VMEM((SUBLANES, lags + depth), jnp.float32),
            pltpu.VMEM((channels, LANES, lags + depth - LANES), jnp.bfloat16),
        ],
        compiler_params=pltpu.CompilerParams(vmem_limit_bytes=VMEM_LIMIT),
        cost_estimate=pl.CostEstimate(flops=1 << 10, transcendentals=0, bytes_accessed=1 << 10),
        name=name,
    )(weighted, *segments)


def first_kernel(token_ref):
    token_ref[...] = jnp.zeros_like(token_ref)


def first():
    return pl.pallas_call(
        first_kernel,
        out_shape=jax.ShapeDtypeStruct((SUBLANES, LANES), jnp.float32),
        out_specs=pl.BlockSpec(memory_space=pltpu.VMEM),
        cost_estimate=pl.CostEstimate(flops=1 << 36, transcendentals=0, bytes_accessed=1 << 26),
        compiler_params=pltpu.CompilerParams(vmem_limit_bytes=1 << 20),
        name="first",
    )()


def add_kernel(*refs):
    total = refs[0][...]
    for ref in refs[1:-1]:
        total = total + ref[...].astype(jnp.float32)
    refs[-1][...] = total


def added(*terms):
    return pl.pallas_call(
        add_kernel,
        out_shape=jax.ShapeDtypeStruct(terms[0].shape, jnp.float32),
        in_specs=[pl.BlockSpec(memory_space=pltpu.VMEM)] * len(terms),
        out_specs=pl.BlockSpec(memory_space=pltpu.VMEM),
        cost_estimate=pl.CostEstimate(flops=1 << 36, transcendentals=0, bytes_accessed=1 << 26),
        compiler_params=pltpu.CompilerParams(vmem_limit_bytes=4 << 20),
        name="added",
    )(*terms)


def local(waveforms, templates, available, usable):
    blocks = lax.axis_size("blk")
    shares = lax.axis_size("sta")
    my_share = lax.axis_index("sta")
    own_rows = available.shape[1] // shares
    chips = shares // 2

    waveforms, token = lax.optimization_barrier((waveforms, first()))
    segments = {0: waveforms}
    for by in range(1, blocks):
        segments[by] = exchanged(waveforms, "blk", by)
    segments = [segments[by] for by in range(blocks)]

    wide, narrow = jnp.float32, jnp.bfloat16
    weighted = weighted_templates(templates, available, usable, token, shares, False)
    mine, other = correlations(weighted, segments, "correlate_leaving")
    summed = (mine + exchanged(other, "sta", 1).astype(wide)).astype(narrow)
    sent = [summed[by * own_rows : (by + 1) * own_rows] for by in range(chips - 1)]
    sent, segments, later = lax.optimization_barrier((sent, segments, token))
    arrived = [
        exchanged(sent[by - 1], "sta", 2 * by)
        for by in sorted(range(1, chips), key=lambda by: -(by ^ (by >> 1)))
    ]
    weighted = weighted_templates(templates, available, usable, later, shares, True)
    mine, other = correlations(weighted, segments, "correlate_staying")
    stacked = added(mine, *arrived) + exchanged(other, "sta", 1).astype(wide)

    station_usable = jnp.sum(usable.reshape(-1, COMPONENTS), axis=1).astype(jnp.float32)
    owned = lax.dynamic_slice_in_dim(available, my_share * own_rows, own_rows, 1)
    counted = jnp.sum(owned.astype(jnp.float32) * station_usable[:, None], axis=0)
    return math.sqrt(TLEN) * stacked * lax.rsqrt(jnp.maximum(counted, 1.0))[:, None]


def solution(mesh):
    return jax.shard_map(
        local,
        mesh=mesh,
        in_specs=(P("sta", "blk"), P("sta", "blk"), P(None, "blk"), P()),
        out_specs=P(("blk", "sta"), None),
        check_vma=False,
    )
```

```python
import functools
import math

import jax
import jax.numpy as jnp
from jax import lax
from jax.experimental import pallas as pl
from jax.experimental.pallas import tpu as pltpu
from jax.sharding import PartitionSpec as P

TLEN = 400
COMPONENTS = 3
LANES = 128
SUBLANES = 8

FLOOR_SHARE = 0.1
EPSILON = 1e-06

PERIOD = LANES // math.gcd(TLEN, LANES)
PERIOD_TILES = PERIOD * TLEN // LANES
DEPTH_TILES = -(-TLEN // LANES)
DEPTH = DEPTH_TILES * LANES
VMEM_LIMIT = 24 << 20


def exchanged(array, axis, by):
    length = lax.axis_size(axis)
    return lax.ppermute(array, axis, [(i, i ^ by) for i in range(length)])


def template_kernel(
    shares, stay, raw_ref, avail_ref, usable_ref, token_ref, *refs
):
    out_ref, *factor_refs, flat, rows, avail_cols = refs
    channels, width = raw_ref.shape
    stations, count = avail_ref.shape
    tiles = width // LANES
    stations_here = channels // COMPONENTS
    own = count // shares
    chips = shares // 2
    chip_rows = 2 * own
    chip_tiles = tiles // chips
    taken = range(1) if stay else range(1, chips)
    groups = len(taken) * chip_rows // PERIOD
    me = lax.axis_index("sta")
    start = me // 2 if stay else me // 2 + 1
    unroll = next(by for by in (25, 20, 16, 10, 8, 5, 4, 2, 1) if chip_tiles % by == 0)

    def spread(step, carry):
        source = lax.rem(start * chip_tiles + step * unroll, tiles)
        for sub in range(unroll):
            value = raw_ref[:, pl.ds(pl.multiple_of((source + sub) * LANES, LANES), LANES)]
            there = pl.multiple_of((step * unroll + sub) * SUBLANES, SUBLANES)
            flat[pl.ds(there, channels), :] = value.astype(jnp.float32)
        return carry

    lax.fori_loop(0, len(taken) * chip_tiles // unroll, spread, 0)

    station_row = lax.broadcasted_iota(jnp.int32, (stations, LANES), 0)
    avail = avail_ref[...].astype(jnp.float32)
    def per_row(by_station):
        return lax.dot_general(
            avail, by_station, (((0,), (0,)), ((), ())), preferred_element_type=jnp.float32
        )

    for factor_ref in factor_refs:
        usable_here = jnp.zeros((stations, LANES), jnp.float32)
        for station in range(stations):
            number = sum(usable_ref[station * COMPONENTS + part] for part in range(COMPONENTS))
            usable_here = jnp.where(station_row == station, number.astype(jnp.float32), usable_here)
        avail_cols[stations_here] = per_row(usable_here)
        counted = avail_cols[stations_here, pl.ds(pl.multiple_of(me * own, own), own), :]
        factor_ref[...] = math.sqrt(TLEN) * lax.rsqrt(jnp.maximum(counted, 1.0))
    for local_station in range(stations_here):
        chosen = station_row == me * stations_here + local_station
        avail_cols[local_station] = per_row(chosen.astype(jnp.float32))

    lane = lax.broadcasted_iota(jnp.int32, (groups, LANES), 1)
    last = TLEN - (DEPTH_TILES - 1) * LANES
    block_lane = lax.broadcasted_iota(jnp.int32, (own, LANES), 1)

    def one_step(step, carry):
        channel = jnp.maximum(step - 1, 0)
        ready = 1 - step % 2
        use = usable_ref[me * channels + channel].astype(jnp.float32)
        for place in range(2 * len(taken)):
            core, chip = divmod(place, len(taken))
            owner = me ^ (2 * taken[chip] + core)
            moved = lax.rem(owner // 2 - start + chips, chips) * chip_rows + owner % 2 * own
            here = pl.ds(pl.multiple_of(moved, own), own)
            parts = [rows[ready, part, here, :] for part in range(DEPTH_TILES)]
            mean = jnp.sum(sum(parts), axis=1, keepdims=True) * (1.0 / TLEN)
            centred = [value - mean for value in parts]
            centred[-1] = jnp.where(block_lane < last, centred[-1], 0.0)
            squared = jnp.sum(sum(value * value for value in centred), axis=1, keepdims=True)
            there = pl.ds(pl.multiple_of(owner * own, own), own)
            weight = avail_cols[channel // COMPONENTS, there, :] * use
            factor = lax.rsqrt(squared + EPSILON) * weight
            for part in range(DEPTH_TILES):
                out_ref[
                    channel, place * own : (place + 1) * own, part * LANES : (part + 1) * LANES
                ] = (centred[part] * factor).astype(jnp.bfloat16)
        channel = jnp.minimum(step, channels - 1)
        filled = step % 2
        for which in range(PERIOD):
            first, offset = divmod(which * TLEN, LANES)
            pieces = []
            for part in range(DEPTH_TILES):
                begin = (first + part) * SUBLANES + channel
                piece = flat[pl.ds(begin, groups, stride=PERIOD_TILES * SUBLANES), :]
                if offset:
                    piece = pltpu.roll(piece, LANES - offset, 1)
                pieces.append(piece)
            for part in range(DEPTH_TILES):
                value = pieces[part]
                if part + 1 < DEPTH_TILES:
                    if offset:
                        value = jnp.where(lane < LANES - offset, value, pieces[part + 1])
                else:
                    value = jnp.where(lane < last, value, 0.0)
                rows[filled, part, pl.ds(which, groups, stride=PERIOD), :] = value
        return carry

    lax.fori_loop(0, channels + 1, one_step, 0)


def weighted_templates(raw, available, usable, token, shares, stay):
    channels, width = raw.shape
    stations, count = available.shape
    taken = 2 * count // shares if stay else count - 2 * count // shares
    outs = [jax.ShapeDtypeStruct((channels, taken, DEPTH), jnp.bfloat16)]
    if stay:
        outs.append(jax.ShapeDtypeStruct((count // shares, LANES), jnp.float32))
    return pl.pallas_call(
        functools.partial(template_kernel, shares, stay),
        out_shape=outs,
        in_specs=[
            pl.BlockSpec(memory_space=pltpu.VMEM),
            pl.BlockSpec(memory_space=pltpu.VMEM),
            pl.BlockSpec(memory_space=pltpu.SMEM),
            pl.BlockSpec(memory_space=pltpu.VMEM),
        ],
        out_specs=[pl.BlockSpec(memory_space=pltpu.VMEM)] * len(outs),
        scratch_shapes=[
            pltpu.VMEM((taken * TLEN // LANES * SUBLANES, LANES), jnp.float32),
            pltpu.VMEM((2, DEPTH_TILES, taken, LANES), jnp.float32),
            pltpu.VMEM((channels // COMPONENTS + 1, count, LANES), jnp.float32),
        ],
        compiler_params=pltpu.CompilerParams(vmem_limit_bytes=VMEM_LIMIT),
        cost_estimate=pl.CostEstimate(flops=1 << 10, transcendentals=0, bytes_accessed=1 << 10),
        name="templates_staying" if stay else "templates_leaving",
    )(raw, available, usable, token)


def ahead(value, by):
    return pltpu.roll(value, value.shape[1] - by, 1) if by else value


def windows_kernel(blocks, *refs):
    segments = refs[:blocks]
    windows, scale, record = refs[blocks:]
    channels, segment = segments[0].shape
    lags = blocks * segment
    wide = record.shape[1]
    base = windows.shape[2]
    me = lax.axis_index("blk")

    record[:, lags:] = jnp.zeros((SUBLANES, wide - lags), jnp.float32)
    for by in range(blocks):
        start = pl.multiple_of((me ^ by) * segment, LANES)
        record[0:channels, pl.ds(start, segment)] = segments[by][...].astype(jnp.float32)

    power = record[...] * record[...]
    energy, taken, span = None, 0, 1
    while True:
        if TLEN & span:
            term = ahead(power, taken)
            energy = term if energy is None else energy + term
            taken += span
        if 2 * span > TLEN:
            break
        power = power + ahead(power, span)
        span *= 2
    scale[...] = lax.rsqrt(jnp.maximum(energy[:, :lags], FLOOR_SHARE * TLEN))

    sublane = lax.broadcasted_iota(jnp.int32, (SUBLANES, wide), 0)

    def one_record(channel, carry):
        shifted = jnp.broadcast_to(record[pl.ds(channel, 1), :], (SUBLANES, wide))
        for bit in (1, 2, 4):
            shifted = jnp.where((sublane & bit) != 0, ahead(shifted, bit), shifted)
        pair = jnp.concatenate([shifted, ahead(shifted, SUBLANES)], axis=0).astype(jnp.bfloat16)
        for row in range(0, LANES, 2 * SUBLANES):
            windows[channel, row : row + 2 * SUBLANES, :] = pair[:, row : row + base]
        return carry

    lax.fori_loop(0, channels, one_record, 0, unroll=2)


def all_windows(segments, name):
    channels, segment = segments[0].shape
    blocks = len(segments)
    lags = blocks * segment
    return pl.pallas_call(
        functools.partial(windows_kernel, blocks),
        out_shape=(
            jax.ShapeDtypeStruct((channels, LANES, lags + DEPTH - LANES), jnp.bfloat16),
            jax.ShapeDtypeStruct((SUBLANES, lags), jnp.float32),
        ),
        in_specs=[pl.BlockSpec(memory_space=pltpu.VMEM)] * blocks,
        out_specs=(pl.BlockSpec(memory_space=pltpu.VMEM),) * 2,
        scratch_shapes=[pltpu.VMEM((SUBLANES, lags + DEPTH), jnp.float32)],
        compiler_params=pltpu.CompilerParams(vmem_limit_bytes=VMEM_LIMIT),
        cost_estimate=pl.CostEstimate(flops=1 << 10, transcendentals=0, bytes_accessed=1 << 10),
        name=name,
    )(*segments)


def correlate_kernel(weighted_ref, windows, scale, *outs):
    channels, count, depth = weighted_ref.shape
    lags = scale.shape[1]
    rows = count // len(outs)
    tile = next(by for by in (16 * LANES, 8 * LANES, 4 * LANES, 2 * LANES) if lags % by == 0)

    def one_tile(first):
        here = pl.ds(first, tile)
        total = None
        for channel in range(channels):
            signal = jnp.concatenate(
                [
                    windows[
                        channel,
                        : min(LANES, TLEN - part * LANES),
                        pl.ds(pl.multiple_of(first + part * LANES, LANES), tile),
                    ]
                    for part in range(depth // LANES)
                ],
                axis=0,
            )
            weights = weighted_ref[channel, :, :TLEN]
            matched = jnp.dot(weights, signal, preferred_element_type=jnp.float32)
            term = matched * scale[channel : channel + 1, here]
            total = term if total is None else total + term
        for place, out in enumerate(outs):
            out[:, here] = total[place * rows : (place + 1) * rows].astype(out.dtype)

    if lags == tile:
        one_tile(0)
    else:

        def one_step(step, carry):
            one_tile(pl.multiple_of(step * tile, LANES))
            return carry

        lax.fori_loop(0, lags // tile, one_step, 0)


def correlations(weighted, windows, scale, blocks, name):
    channels, count, depth = weighted.shape
    lags = scale.shape[1]
    kinds = [jnp.float32] * (blocks // 2) + [jnp.bfloat16] * (blocks // 2)
    return pl.pallas_call(
        correlate_kernel,
        out_shape=[jax.ShapeDtypeStruct((count // blocks, lags), kind) for kind in kinds],
        in_specs=[pl.BlockSpec(memory_space=pltpu.VMEM)] * 3,
        out_specs=[pl.BlockSpec(memory_space=pltpu.VMEM)] * blocks,
        compiler_params=pltpu.CompilerParams(vmem_limit_bytes=VMEM_LIMIT),
        cost_estimate=pl.CostEstimate(flops=1 << 10, transcendentals=0, bytes_accessed=1 << 10),
        name=name,
    )(weighted, windows, scale)


def first_kernel(token_ref):
    token_ref[...] = jnp.zeros_like(token_ref)


def first():
    return pl.pallas_call(
        first_kernel,
        out_shape=jax.ShapeDtypeStruct((SUBLANES, LANES), jnp.float32),
        out_specs=pl.BlockSpec(memory_space=pltpu.VMEM),
        cost_estimate=pl.CostEstimate(flops=1 << 36, transcendentals=0, bytes_accessed=1 << 26),
        compiler_params=pltpu.CompilerParams(vmem_limit_bytes=1 << 20),
        name="first",
    )()


def add_kernel(*refs):
    total = refs[0][...]
    for ref in refs[1:-1]:
        total = total + ref[...].astype(jnp.float32)
    refs[-1][...] = total


def added(*terms):
    return pl.pallas_call(
        add_kernel,
        out_shape=jax.ShapeDtypeStruct(terms[0].shape, jnp.float32),
        in_specs=[pl.BlockSpec(memory_space=pltpu.VMEM)] * len(terms),
        out_specs=pl.BlockSpec(memory_space=pltpu.VMEM),
        cost_estimate=pl.CostEstimate(flops=1 << 36, transcendentals=0, bytes_accessed=1 << 26),
        compiler_params=pltpu.CompilerParams(vmem_limit_bytes=4 << 20),
        name="added",
    )(*terms)


def scale_kernel(factor_ref, *refs):
    factor = factor_ref[...]
    for start in range(0, refs[-1].shape[1], LANES):
        here = slice(start, start + LANES)
        total = refs[0][:, here]
        for ref in refs[1:-1]:
            total = total + ref[:, here].astype(jnp.float32)
        refs[-1][:, here] = total * factor


def scaled(factor, *terms):
    return pl.pallas_call(
        scale_kernel,
        out_shape=jax.ShapeDtypeStruct(terms[0].shape, jnp.float32),
        in_specs=[pl.BlockSpec(memory_space=pltpu.VMEM)] * (1 + len(terms)),
        out_specs=pl.BlockSpec(memory_space=pltpu.VMEM),
        compiler_params=pltpu.CompilerParams(vmem_limit_bytes=4 << 20),
        cost_estimate=pl.CostEstimate(flops=1 << 10, transcendentals=0, bytes_accessed=1 << 10),
        name="scaled",
    )(factor, *terms)


def local(waveforms, templates, available, usable):
    blocks = lax.axis_size("blk")
    shares = lax.axis_size("sta")
    chips = shares // 2

    waveforms, token = lax.optimization_barrier((waveforms, first()))
    segments = {0: waveforms}
    for by in range(1, blocks):
        segments[by] = exchanged(waveforms, "blk", by)
    segments = [segments[by] for by in range(blocks)]

    wide, narrow = jnp.float32, jnp.bfloat16
    (weighted,) = weighted_templates(templates, available, usable, token, shares, False)
    windows, scale = all_windows(segments, "windows")
    sums = correlations(weighted, windows, scale, 2 * (chips - 1), "correlate_leaving")
    order = sorted(range(1, chips), key=lambda by: -(by ^ (by >> 1)))
    partner = {by: exchanged(sums[chips - 1 + by - 1], "sta", 1) for by in order}
    sent = []
    for by in order:
        own = sums[by - 1]
        if sent:
            own, sent[-1] = lax.optimization_barrier((own, sent[-1]))
        sent.append((own + partner[by].astype(wide)).astype(narrow))
    sent[-1], scale, later = lax.optimization_barrier((sent[-1], scale, token))
    arrived = [exchanged(term, "sta", 2 * by) for by, term in zip(order, sent)]

    weighted, factor = weighted_templates(templates, available, usable, later, shares, True)
    mine, other = correlations(weighted, windows, scale, 2, "correlate_staying")
    return scaled(factor, added(mine, *arrived), exchanged(other, "sta", 1))


def solution(mesh):
    return jax.shard_map(
        local,
        mesh=mesh,
        in_specs=(P("sta", "blk"), P("sta", "blk"), P(None, "blk"), P()),
        out_specs=P(("blk", "sta"), None),
        check_vma=False,
    )
```

```python
import functools
import math

import jax
import jax.numpy as jnp
from jax import lax
from jax.experimental import pallas as pl
from jax.experimental.pallas import tpu as pltpu
from jax.sharding import PartitionSpec as P

TLEN = 400
COMPONENTS = 3
LANES = 128
SUBLANES = 8

FLOOR_SHARE = 0.1
EPSILON = 1e-06

PERIOD = LANES // math.gcd(TLEN, LANES)
PERIOD_TILES = PERIOD * TLEN // LANES
DEPTH_TILES = -(-TLEN // LANES)
DEPTH = DEPTH_TILES * LANES
VMEM_LIMIT = 24 << 20


def exchanged(array, axis, by):
    length = lax.axis_size(axis)
    return lax.ppermute(array, axis, [(i, i ^ by) for i in range(length)])


def template_kernel(
    shares, stay, raw_ref, avail_ref, usable_ref, token_ref, *refs
):
    out_ref, *factor_refs, rows, avail_cols = refs
    channels, width = raw_ref.shape
    stations, count = avail_ref.shape
    tiles = width // LANES
    stations_here = channels // COMPONENTS
    own = count // shares
    chips = shares // 2
    chip_rows = 2 * own
    chip_tiles = tiles // chips
    taken = range(1) if stay else range(1, chips)
    groups = len(taken) * chip_rows // PERIOD
    me = lax.axis_index("sta")
    start = me // 2 if stay else me // 2 + 1
    last = TLEN - (DEPTH_TILES - 1) * LANES
    lane = lax.broadcasted_iota(jnp.int32, (channels, LANES), 1)

    def one_group(group, carry):
        source = lax.rem(start * chip_tiles + group * PERIOD_TILES, tiles)
        for which in range(PERIOD):
            first, offset = divmod(which * TLEN, LANES)
            pieces = []
            for part in range(DEPTH_TILES):
                begin = pl.multiple_of((source + first + part) * LANES, LANES)
                piece = raw_ref[:, pl.ds(begin, LANES)].astype(jnp.float32)
                if offset:
                    piece = pltpu.roll(piece, LANES - offset, 1)
                pieces.append(piece)
            row = pl.multiple_of((group * PERIOD + which) * SUBLANES, SUBLANES)
            for part in range(DEPTH_TILES):
                value = pieces[part]
                if part + 1 < DEPTH_TILES:
                    if offset:
                        value = jnp.where(lane < LANES - offset, value, pieces[part + 1])
                else:
                    value = jnp.where(lane < last, value, 0.0)
                rows[part, pl.ds(row, channels), :] = value
        return carry

    lax.fori_loop(0, groups, one_group, 0, unroll=8)

    station_row = lax.broadcasted_iota(jnp.int32, (stations, LANES), 0)
    avail = avail_ref[...].astype(jnp.float32)
    def per_row(by_station):
        return lax.dot_general(
            avail, by_station, (((0,), (0,)), ((), ())), preferred_element_type=jnp.float32
        )

    for factor_ref in factor_refs:
        usable_here = jnp.zeros((stations, LANES), jnp.float32)
        for station in range(stations):
            number = sum(usable_ref[station * COMPONENTS + part] for part in range(COMPONENTS))
            usable_here = jnp.where(station_row == station, number.astype(jnp.float32), usable_here)
        avail_cols[stations_here] = per_row(usable_here)
        counted = avail_cols[stations_here, pl.ds(pl.multiple_of(me * own, own), own), :]
        factor_ref[...] = math.sqrt(TLEN) * lax.rsqrt(jnp.maximum(counted, 1.0))
    for local_station in range(stations_here):
        chosen = station_row == me * stations_here + local_station
        avail_cols[local_station] = per_row(chosen.astype(jnp.float32))

    block_lane = lax.broadcasted_iota(jnp.int32, (own, LANES), 1)

    def one_channel(channel, carry):
        use = usable_ref[me * channels + channel].astype(jnp.float32)
        for place in range(2 * len(taken)):
            core, chip = divmod(place, len(taken))
            owner = me ^ (2 * taken[chip] + core)
            moved = lax.rem(owner // 2 - start + chips, chips) * chip_rows + owner % 2 * own
            here = pl.ds(moved * SUBLANES + channel, own, stride=SUBLANES)
            parts = [rows[part, here, :] for part in range(DEPTH_TILES)]
            mean = jnp.sum(sum(parts), axis=1, keepdims=True) * (1.0 / TLEN)
            centred = [value - mean for value in parts]
            centred[-1] = jnp.where(block_lane < last, centred[-1], 0.0)
            squared = jnp.sum(sum(value * value for value in centred), axis=1, keepdims=True)
            there = pl.ds(pl.multiple_of(owner * own, own), own)
            weight = avail_cols[channel // COMPONENTS, there, :] * use
            factor = lax.rsqrt(squared + EPSILON) * weight
            for part in range(DEPTH_TILES):
                out_ref[
                    channel, place * own : (place + 1) * own, part * LANES : (part + 1) * LANES
                ] = (centred[part] * factor).astype(jnp.bfloat16)
        return carry

    lax.fori_loop(0, channels, one_channel, 0, unroll=2)


def weighted_templates(raw, available, usable, token, shares, stay):
    channels, width = raw.shape
    stations, count = available.shape
    taken = 2 * count // shares if stay else count - 2 * count // shares
    outs = [jax.ShapeDtypeStruct((channels, taken, DEPTH), jnp.bfloat16)]
    if stay:
        outs.append(jax.ShapeDtypeStruct((count // shares, LANES), jnp.float32))
    return pl.pallas_call(
        functools.partial(template_kernel, shares, stay),
        out_shape=outs,
        in_specs=[
            pl.BlockSpec(memory_space=pltpu.VMEM),
            pl.BlockSpec(memory_space=pltpu.VMEM),
            pl.BlockSpec(memory_space=pltpu.SMEM),
            pl.BlockSpec(memory_space=pltpu.VMEM),
        ],
        out_specs=[pl.BlockSpec(memory_space=pltpu.VMEM)] * len(outs),
        scratch_shapes=[
            pltpu.VMEM((DEPTH_TILES, taken * SUBLANES, LANES), jnp.float32),
            pltpu.VMEM((channels // COMPONENTS + 1, count, LANES), jnp.float32),
        ],
        compiler_params=pltpu.CompilerParams(vmem_limit_bytes=VMEM_LIMIT),
        cost_estimate=pl.CostEstimate(flops=1 << 10, transcendentals=0, bytes_accessed=1 << 10),
        name="templates_staying" if stay else "templates_leaving",
    )(raw, available, usable, token)


def ahead(value, by):
    return pltpu.roll(value, value.shape[1] - by, 1) if by else value


def windows_kernel(blocks, *refs):
    segments = refs[:blocks]
    windows, scale, record = refs[blocks:]
    channels, segment = segments[0].shape
    lags = blocks * segment
    wide = record.shape[1]
    base = windows.shape[2]
    me = lax.axis_index("blk")

    record[:, lags:] = jnp.zeros((SUBLANES, wide - lags), jnp.float32)
    for by in range(blocks):
        start = pl.multiple_of((me ^ by) * segment, LANES)
        record[0:channels, pl.ds(start, segment)] = segments[by][...].astype(jnp.float32)

    power = record[...] * record[...]
    energy, taken, span = None, 0, 1
    while True:
        if TLEN & span:
            term = ahead(power, taken)
            energy = term if energy is None else energy + term
            taken += span
        if 2 * span > TLEN:
            break
        power = power + ahead(power, span)
        span *= 2
    scale[...] = lax.rsqrt(jnp.maximum(energy[:, :lags], FLOOR_SHARE * TLEN))

    sublane = lax.broadcasted_iota(jnp.int32, (SUBLANES, wide), 0)

    def one_record(channel, carry):
        shifted = jnp.broadcast_to(record[pl.ds(channel, 1), :], (SUBLANES, wide))
        for bit in (1, 2, 4):
            shifted = jnp.where((sublane & bit) != 0, ahead(shifted, bit), shifted)
        pair = jnp.concatenate([shifted, ahead(shifted, SUBLANES)], axis=0).astype(jnp.bfloat16)
        for row in range(0, LANES, 2 * SUBLANES):
            windows[channel, row : row + 2 * SUBLANES, :] = pair[:, row : row + base]
        return carry

    lax.fori_loop(0, channels, one_record, 0, unroll=2)


def all_windows(segments, name):
    channels, segment = segments[0].shape
    blocks = len(segments)
    lags = blocks * segment
    return pl.pallas_call(
        functools.partial(windows_kernel, blocks),
        out_shape=(
            jax.ShapeDtypeStruct((channels, LANES, lags + DEPTH - LANES), jnp.bfloat16),
            jax.ShapeDtypeStruct((SUBLANES, lags), jnp.float32),
        ),
        in_specs=[pl.BlockSpec(memory_space=pltpu.VMEM)] * blocks,
        out_specs=(pl.BlockSpec(memory_space=pltpu.VMEM),) * 2,
        scratch_shapes=[pltpu.VMEM((SUBLANES, lags + DEPTH), jnp.float32)],
        compiler_params=pltpu.CompilerParams(vmem_limit_bytes=VMEM_LIMIT),
        cost_estimate=pl.CostEstimate(flops=1 << 10, transcendentals=0, bytes_accessed=1 << 10),
        name=name,
    )(*segments)


def correlate_kernel(weighted_ref, windows, scale, *outs):
    channels, count, depth = weighted_ref.shape
    lags = scale.shape[1]
    rows = count // len(outs)
    tile = next(by for by in (16 * LANES, 8 * LANES, 4 * LANES, 2 * LANES) if lags % by == 0)

    def one_tile(first):
        here = pl.ds(first, tile)
        total = None
        for channel in range(channels):
            signal = jnp.concatenate(
                [
                    windows[
                        channel,
                        : min(LANES, TLEN - part * LANES),
                        pl.ds(pl.multiple_of(first + part * LANES, LANES), tile),
                    ]
                    for part in range(depth // LANES)
                ],
                axis=0,
            )
            weights = weighted_ref[channel, :, :TLEN]
            matched = jnp.dot(weights, signal, preferred_element_type=jnp.float32)
            term = matched * scale[channel : channel + 1, here]
            total = term if total is None else total + term
        for place, out in enumerate(outs):
            out[:, here] = total[place * rows : (place + 1) * rows].astype(out.dtype)

    if lags == tile:
        one_tile(0)
    else:

        def one_step(step, carry):
            one_tile(pl.multiple_of(step * tile, LANES))
            return carry

        lax.fori_loop(0, lags // tile, one_step, 0)


def correlations(weighted, windows, scale, blocks, name):
    channels, count, depth = weighted.shape
    lags = scale.shape[1]
    kinds = [jnp.float32] * (blocks // 2) + [jnp.bfloat16] * (blocks // 2)
    return pl.pallas_call(
        correlate_kernel,
        out_shape=[jax.ShapeDtypeStruct((count // blocks, lags), kind) for kind in kinds],
        in_specs=[pl.BlockSpec(memory_space=pltpu.VMEM)] * 3,
        out_specs=[pl.BlockSpec(memory_space=pltpu.VMEM)] * blocks,
        compiler_params=pltpu.CompilerParams(vmem_limit_bytes=VMEM_LIMIT),
        cost_estimate=pl.CostEstimate(flops=1 << 10, transcendentals=0, bytes_accessed=1 << 10),
        name=name,
    )(weighted, windows, scale)


def first_kernel(token_ref):
    token_ref[...] = jnp.zeros_like(token_ref)


def first():
    return pl.pallas_call(
        first_kernel,
        out_shape=jax.ShapeDtypeStruct((SUBLANES, LANES), jnp.float32),
        out_specs=pl.BlockSpec(memory_space=pltpu.VMEM),
        cost_estimate=pl.CostEstimate(flops=1 << 36, transcendentals=0, bytes_accessed=1 << 26),
        compiler_params=pltpu.CompilerParams(vmem_limit_bytes=1 << 20),
        name="first",
    )()


def add_kernel(*refs):
    total = refs[0][...]
    for ref in refs[1:-1]:
        total = total + ref[...].astype(jnp.float32)
    refs[-1][...] = total


def added(*terms):
    return pl.pallas_call(
        add_kernel,
        out_shape=jax.ShapeDtypeStruct(terms[0].shape, jnp.float32),
        in_specs=[pl.BlockSpec(memory_space=pltpu.VMEM)] * len(terms),
        out_specs=pl.BlockSpec(memory_space=pltpu.VMEM),
        cost_estimate=pl.CostEstimate(flops=1 << 36, transcendentals=0, bytes_accessed=1 << 26),
        compiler_params=pltpu.CompilerParams(vmem_limit_bytes=4 << 20),
        name="added",
    )(*terms)


def scale_kernel(factor_ref, *refs):
    factor = factor_ref[...]
    for start in range(0, refs[-1].shape[1], LANES):
        here = slice(start, start + LANES)
        total = refs[0][:, here]
        for ref in refs[1:-1]:
            total = total + ref[:, here].astype(jnp.float32)
        refs[-1][:, here] = total * factor


def scaled(factor, *terms):
    return pl.pallas_call(
        scale_kernel,
        out_shape=jax.ShapeDtypeStruct(terms[0].shape, jnp.float32),
        in_specs=[pl.BlockSpec(memory_space=pltpu.VMEM)] * (1 + len(terms)),
        out_specs=pl.BlockSpec(memory_space=pltpu.VMEM),
        compiler_params=pltpu.CompilerParams(vmem_limit_bytes=4 << 20),
        cost_estimate=pl.CostEstimate(flops=1 << 10, transcendentals=0, bytes_accessed=1 << 10),
        name="scaled",
    )(factor, *terms)


def local(waveforms, templates, available, usable):
    blocks = lax.axis_size("blk")
    shares = lax.axis_size("sta")
    chips = shares // 2

    waveforms, token = lax.optimization_barrier((waveforms, first()))
    segments = {0: waveforms}
    for by in range(1, blocks):
        segments[by] = exchanged(waveforms, "blk", by)
    segments = [segments[by] for by in range(blocks)]

    wide, narrow = jnp.float32, jnp.bfloat16
    (weighted,) = weighted_templates(templates, available, usable, token, shares, False)
    windows, scale = all_windows(segments, "windows")
    sums = correlations(weighted, windows, scale, 2 * (chips - 1), "correlate_leaving")
    order = sorted(range(1, chips), key=lambda by: -(by ^ (by >> 1)))
    partner = {by: exchanged(sums[chips - 1 + by - 1], "sta", 1) for by in order}
    sent = []
    for by in order:
        own = sums[by - 1]
        if sent:
            own, sent[-1] = lax.optimization_barrier((own, sent[-1]))
        sent.append((own + partner[by].astype(wide)).astype(narrow))
    sent[-1], scale, later = lax.optimization_barrier((sent[-1], scale, token))
    arrived = [exchanged(term, "sta", 2 * by) for by, term in zip(order, sent)]

    weighted, factor = weighted_templates(templates, available, usable, later, shares, True)
    mine, other = correlations(weighted, windows, scale, 2, "correlate_staying")
    return scaled(factor, added(mine, *arrived), exchanged(other, "sta", 1))


def solution(mesh):
    return jax.shard_map(
        local,
        mesh=mesh,
        in_specs=(P("sta", "blk"), P("sta", "blk"), P(None, "blk"), P()),
        out_specs=P(("blk", "sta"), None),
        check_vma=False,
    )
```

```python
import functools
import math

import jax
import jax.numpy as jnp
from jax import lax
from jax.experimental import pallas as pl
from jax.experimental.pallas import tpu as pltpu
from jax.sharding import PartitionSpec as P

TLEN = 400
COMPONENTS = 3
LANES = 128
SUBLANES = 8

FLOOR_SHARE = 0.1
EPSILON = 1e-06

PERIOD = LANES // math.gcd(TLEN, LANES)
PERIOD_TILES = PERIOD * TLEN // LANES
DEPTH_TILES = -(-TLEN // LANES)
DEPTH = DEPTH_TILES * LANES
VMEM_LIMIT = 24 << 20


def exchanged(array, axis, by):
    length = lax.axis_size(axis)
    return lax.ppermute(array, axis, [(i, i ^ by) for i in range(length)])


def template_kernel(
    shares, stay, raw_ref, avail_ref, usable_ref, token_ref, *refs
):
    out_ref, *factor_refs, rows, avail_cols = refs
    channels, width = raw_ref.shape
    stations, count = avail_ref.shape
    tiles = width // LANES
    stations_here = channels // COMPONENTS
    own = count // shares
    chips = shares // 2
    chip_rows = 2 * own
    chip_tiles = tiles // chips
    taken = range(1) if stay else range(1, chips)
    groups = len(taken) * chip_rows // PERIOD
    me = lax.axis_index("sta")
    start = me // 2 if stay else me // 2 + 1
    last = TLEN - (DEPTH_TILES - 1) * LANES
    lane = lax.broadcasted_iota(jnp.int32, (channels, LANES), 1)

    def one_group(group, carry):
        source = lax.rem(start * chip_tiles + group * PERIOD_TILES, tiles)
        for which in range(PERIOD):
            first, offset = divmod(which * TLEN, LANES)
            pieces = []
            for part in range(DEPTH_TILES):
                begin = pl.multiple_of((source + first + part) * LANES, LANES)
                piece = raw_ref[:, pl.ds(begin, LANES)].astype(jnp.float32)
                if offset:
                    piece = pltpu.roll(piece, LANES - offset, 1)
                pieces.append(piece)
            row = pl.multiple_of((group * PERIOD + which) * SUBLANES, SUBLANES)
            for part in range(DEPTH_TILES):
                value = pieces[part]
                if part + 1 < DEPTH_TILES:
                    if offset:
                        value = jnp.where(lane < LANES - offset, value, pieces[part + 1])
                else:
                    value = jnp.where(lane < last, value, 0.0)
                rows[part, pl.ds(row, channels), :] = value
        return carry

    lax.fori_loop(0, groups, one_group, 0, unroll=8)

    station_row = lax.broadcasted_iota(jnp.int32, (stations, LANES), 0)
    avail = avail_ref[...].astype(jnp.float32)
    def per_row(by_station):
        return lax.dot_general(
            avail, by_station, (((0,), (0,)), ((), ())), preferred_element_type=jnp.float32
        )

    for factor_ref in factor_refs:
        usable_here = jnp.zeros((stations, LANES), jnp.float32)
        for station in range(stations):
            number = sum(usable_ref[station * COMPONENTS + part] for part in range(COMPONENTS))
            usable_here = jnp.where(station_row == station, number.astype(jnp.float32), usable_here)
        avail_cols[stations_here] = per_row(usable_here)
        counted = avail_cols[stations_here, pl.ds(pl.multiple_of(me * own, own), own), :]
        factor_ref[...] = math.sqrt(TLEN) * lax.rsqrt(jnp.maximum(counted, 1.0))
    for local_station in range(stations_here):
        chosen = station_row == me * stations_here + local_station
        avail_cols[local_station] = per_row(chosen.astype(jnp.float32))

    block_lane = lax.broadcasted_iota(jnp.int32, (own, LANES), 1)

    def one_channel(channel, carry):
        use = usable_ref[me * channels + channel].astype(jnp.float32)
        for place in range(2 * len(taken)):
            core, chip = divmod(place, len(taken))
            owner = me ^ (2 * taken[chip] + core)
            moved = lax.rem(owner // 2 - start + chips, chips) * chip_rows + owner % 2 * own
            here = pl.ds(moved * SUBLANES + channel, own, stride=SUBLANES)
            parts = [rows[part, here, :] for part in range(DEPTH_TILES)]
            mean = jnp.sum(sum(parts), axis=1, keepdims=True) * (1.0 / TLEN)
            centred = [value - mean for value in parts]
            centred[-1] = jnp.where(block_lane < last, centred[-1], 0.0)
            squared = jnp.sum(sum(value * value for value in centred), axis=1, keepdims=True)
            there = pl.ds(pl.multiple_of(owner * own, own), own)
            weight = avail_cols[channel // COMPONENTS, there, :] * use
            factor = lax.rsqrt(squared + EPSILON) * weight
            for part in range(DEPTH_TILES):
                out_ref[
                    channel, place * own : (place + 1) * own, part * LANES : (part + 1) * LANES
                ] = (centred[part] * factor).astype(jnp.bfloat16)
        return carry

    lax.fori_loop(0, channels, one_channel, 0, unroll=2)


def weighted_templates(raw, available, usable, token, shares, stay):
    channels, width = raw.shape
    stations, count = available.shape
    taken = 2 * count // shares if stay else count - 2 * count // shares
    outs = [jax.ShapeDtypeStruct((channels, taken, DEPTH), jnp.bfloat16)]
    if stay:
        outs.append(jax.ShapeDtypeStruct((count // shares, LANES), jnp.float32))
    return pl.pallas_call(
        functools.partial(template_kernel, shares, stay),
        out_shape=outs,
        in_specs=[
            pl.BlockSpec(memory_space=pltpu.VMEM),
            pl.BlockSpec(memory_space=pltpu.VMEM),
            pl.BlockSpec(memory_space=pltpu.SMEM),
            pl.BlockSpec(memory_space=pltpu.VMEM),
        ],
        out_specs=[pl.BlockSpec(memory_space=pltpu.VMEM)] * len(outs),
        scratch_shapes=[
            pltpu.VMEM((DEPTH_TILES, taken * SUBLANES, LANES), jnp.float32),
            pltpu.VMEM((channels // COMPONENTS + 1, count, LANES), jnp.float32),
        ],
        compiler_params=pltpu.CompilerParams(vmem_limit_bytes=VMEM_LIMIT),
        cost_estimate=pl.CostEstimate(flops=1 << 10, transcendentals=0, bytes_accessed=1 << 10),
        name="templates_staying" if stay else "templates_leaving",
    )(raw, available, usable, token)


def ahead(value, by):
    return pltpu.roll(value, value.shape[1] - by, 1) if by else value


def windows_kernel(blocks, *refs):
    segments = refs[:blocks]
    windows, scale, record, starts = refs[blocks:]
    channels, segment = segments[0].shape
    lags = blocks * segment
    wide = record.shape[1]
    base = windows.shape[2]
    me = lax.axis_index("blk")

    record[:, lags:] = jnp.zeros((SUBLANES, wide - lags), jnp.float32)
    for by in range(blocks):
        start = pl.multiple_of((me ^ by) * segment, LANES)
        record[0:channels, pl.ds(start, segment)] = segments[by][...].astype(jnp.float32)

    sums = {1: record[...] * record[...]}
    span = 1
    while 2 * span <= TLEN:
        sums[2 * span] = sums[span] + ahead(sums[span], span)
        span *= 2
    energy, taken = None, 0
    while taken < TLEN:
        if taken + span <= TLEN:
            term = sums[span][:, taken : taken + lags]
            energy = term if energy is None else energy + term
            taken += span
        span //= 2
    scale[...] = lax.rsqrt(jnp.maximum(energy, FLOOR_SHARE * TLEN))

    sublane = lax.broadcasted_iota(jnp.int32, (SUBLANES, wide), 0)
    for channel in range(channels):
        shifted = jnp.broadcast_to(record[channel : channel + 1, :], (SUBLANES, wide))
        for bit in (1, 2, 4):
            shifted = jnp.where((sublane & bit) != 0, ahead(shifted, bit), shifted)
        pair = jnp.concatenate([shifted, ahead(shifted, SUBLANES)], axis=0).astype(jnp.bfloat16)
        starts[channel] = pair
        windows[channel, : 2 * SUBLANES, :] = pair[:, :base]

    def one_channel(channel, carry):
        pair = starts[channel]
        for row in range(2 * SUBLANES, LANES, 2 * SUBLANES):
            windows[channel, row : row + 2 * SUBLANES, :] = pair[:, row : row + base]
        return carry

    lax.fori_loop(0, channels, one_channel, 0, unroll=3)


def all_windows(segments, name):
    channels, segment = segments[0].shape
    blocks = len(segments)
    lags = blocks * segment
    return pl.pallas_call(
        functools.partial(windows_kernel, blocks),
        out_shape=(
            jax.ShapeDtypeStruct((channels, LANES, lags + DEPTH - LANES), jnp.bfloat16),
            jax.ShapeDtypeStruct((SUBLANES, lags), jnp.float32),
        ),
        in_specs=[pl.BlockSpec(memory_space=pltpu.VMEM)] * blocks,
        out_specs=(pl.BlockSpec(memory_space=pltpu.VMEM),) * 2,
        scratch_shapes=[
            pltpu.VMEM((SUBLANES, lags + DEPTH), jnp.float32),
            pltpu.VMEM((channels, 2 * SUBLANES, lags + DEPTH), jnp.bfloat16),
        ],
        compiler_params=pltpu.CompilerParams(vmem_limit_bytes=VMEM_LIMIT),
        cost_estimate=pl.CostEstimate(flops=1 << 10, transcendentals=0, bytes_accessed=1 << 10),
        name=name,
    )(*segments)


def correlate_kernel(weighted_ref, windows, scale, *outs):
    channels, count, depth = weighted_ref.shape
    lags = scale.shape[1]
    rows = count // len(outs)
    tile = next(by for by in (16 * LANES, 8 * LANES, 4 * LANES, 2 * LANES) if lags % by == 0)

    def one_tile(first):
        here = pl.ds(first, tile)
        total = None
        for channel in range(channels):
            signal = jnp.concatenate(
                [
                    windows[
                        channel,
                        : min(LANES, TLEN - part * LANES),
                        pl.ds(pl.multiple_of(first + part * LANES, LANES), tile),
                    ]
                    for part in range(depth // LANES)
                ],
                axis=0,
            )
            weights = weighted_ref[channel, :, :TLEN]
            matched = jnp.dot(weights, signal, preferred_element_type=jnp.float32)
            term = matched * scale[channel : channel + 1, here]
            total = term if total is None else total + term
        for place, out in enumerate(outs):
            out[:, here] = total[place * rows : (place + 1) * rows].astype(out.dtype)

    if lags == tile:
        one_tile(0)
    else:

        def one_step(step, carry):
            one_tile(pl.multiple_of(step * tile, LANES))
            return carry

        lax.fori_loop(0, lags // tile, one_step, 0)


def correlations(weighted, windows, scale, blocks, name):
    channels, count, depth = weighted.shape
    lags = scale.shape[1]
    kinds = [jnp.float32] * (blocks // 2) + [jnp.bfloat16] * (blocks // 2)
    return pl.pallas_call(
        correlate_kernel,
        out_shape=[jax.ShapeDtypeStruct((count // blocks, lags), kind) for kind in kinds],
        in_specs=[pl.BlockSpec(memory_space=pltpu.VMEM)] * 3,
        out_specs=[pl.BlockSpec(memory_space=pltpu.VMEM)] * blocks,
        compiler_params=pltpu.CompilerParams(vmem_limit_bytes=VMEM_LIMIT),
        cost_estimate=pl.CostEstimate(flops=1 << 10, transcendentals=0, bytes_accessed=1 << 10),
        name=name,
    )(weighted, windows, scale)


def first_kernel(token_ref):
    token_ref[...] = jnp.zeros_like(token_ref)


def first():
    return pl.pallas_call(
        first_kernel,
        out_shape=jax.ShapeDtypeStruct((SUBLANES, LANES), jnp.float32),
        out_specs=pl.BlockSpec(memory_space=pltpu.VMEM),
        cost_estimate=pl.CostEstimate(flops=1 << 36, transcendentals=0, bytes_accessed=1 << 26),
        compiler_params=pltpu.CompilerParams(vmem_limit_bytes=1 << 20),
        name="first",
    )()


def add_kernel(*refs):
    total = refs[0][...]
    for ref in refs[1:-1]:
        total = total + ref[...].astype(jnp.float32)
    refs[-1][...] = total


def added(*terms):
    return pl.pallas_call(
        add_kernel,
        out_shape=jax.ShapeDtypeStruct(terms[0].shape, jnp.float32),
        in_specs=[pl.BlockSpec(memory_space=pltpu.VMEM)] * len(terms),
        out_specs=pl.BlockSpec(memory_space=pltpu.VMEM),
        cost_estimate=pl.CostEstimate(flops=1 << 36, transcendentals=0, bytes_accessed=1 << 26),
        compiler_params=pltpu.CompilerParams(vmem_limit_bytes=4 << 20),
        name="added",
    )(*terms)


def scale_kernel(factor_ref, *refs):
    factor = factor_ref[...]
    for start in range(0, refs[-1].shape[1], LANES):
        here = slice(start, start + LANES)
        total = refs[0][:, here]
        for ref in refs[1:-1]:
            total = total + ref[:, here].astype(jnp.float32)
        refs[-1][:, here] = total * factor


def scaled(factor, *terms):
    return pl.pallas_call(
        scale_kernel,
        out_shape=jax.ShapeDtypeStruct(terms[0].shape, jnp.float32),
        in_specs=[pl.BlockSpec(memory_space=pltpu.VMEM)] * (1 + len(terms)),
        out_specs=pl.BlockSpec(memory_space=pltpu.VMEM),
        compiler_params=pltpu.CompilerParams(vmem_limit_bytes=4 << 20),
        cost_estimate=pl.CostEstimate(flops=1 << 10, transcendentals=0, bytes_accessed=1 << 10),
        name="scaled",
    )(factor, *terms)


def local(waveforms, templates, available, usable):
    blocks = lax.axis_size("blk")
    shares = lax.axis_size("sta")
    chips = shares // 2

    waveforms, token = lax.optimization_barrier((waveforms, first()))
    segments = {0: waveforms}
    for by in range(1, blocks):
        segments[by] = exchanged(waveforms, "blk", by)
    segments = [segments[by] for by in range(blocks)]

    wide, narrow = jnp.float32, jnp.bfloat16
    (weighted,) = weighted_templates(templates, available, usable, token, shares, False)
    windows, scale = all_windows(segments, "windows")
    sums = correlations(weighted, windows, scale, 2 * (chips - 1), "correlate_leaving")
    order = sorted(range(1, chips), key=lambda by: -(by ^ (by >> 1)))
    partner = {by: exchanged(sums[chips - 1 + by - 1], "sta", 1) for by in order}
    sent = []
    for by in order:
        own = sums[by - 1]
        if sent:
            own, sent[-1] = lax.optimization_barrier((own, sent[-1]))
        sent.append((own + partner[by].astype(wide)).astype(narrow))
    sent[-1], scale, later = lax.optimization_barrier((sent[-1], scale, token))
    arrived = [exchanged(term, "sta", 2 * by) for by, term in zip(order, sent)]

    weighted, factor = weighted_templates(templates, available, usable, later, shares, True)
    mine, other = correlations(weighted, windows, scale, 2, "correlate_staying")
    return scaled(factor, added(mine, *arrived), exchanged(other, "sta", 1))


def solution(mesh):
    return jax.shard_map(
        local,
        mesh=mesh,
        in_specs=(P("sta", "blk"), P("sta", "blk"), P(None, "blk"), P()),
        out_specs=P(("blk", "sta"), None),
        check_vma=False,
    )
```

```python
import functools
import math

import jax
import jax.numpy as jnp
from jax import lax
from jax.experimental import pallas as pl
from jax.experimental.pallas import tpu as pltpu
from jax.sharding import PartitionSpec as P

TLEN = 400
COMPONENTS = 3
LANES = 128
SUBLANES = 8

FLOOR_SHARE = 0.1
EPSILON = 1e-06

PERIOD = LANES // math.gcd(TLEN, LANES)
PERIOD_TILES = PERIOD * TLEN // LANES
DEPTH_TILES = -(-TLEN // LANES)
DEPTH = DEPTH_TILES * LANES
VMEM_LIMIT = 24 << 20


def exchanged(array, axis, by):
    length = lax.axis_size(axis)
    return lax.ppermute(array, axis, [(i, i ^ by) for i in range(length)])


def template_kernel(
    shares, stay, raw_ref, avail_ref, usable_ref, token_ref, *refs
):
    out_ref, *factor_refs, rows, avail_cols = refs
    channels, width = raw_ref.shape
    stations, count = avail_ref.shape
    tiles = width // LANES
    stations_here = channels // COMPONENTS
    own = count // shares
    chips = shares // 2
    chip_rows = 2 * own
    chip_tiles = tiles // chips
    taken = range(1) if stay else range(1, chips)
    groups = len(taken) * chip_rows // PERIOD
    me = lax.axis_index("sta")
    start = me // 2 if stay else me // 2 + 1
    last = TLEN - (DEPTH_TILES - 1) * LANES
    lane = lax.broadcasted_iota(jnp.int32, (channels, LANES), 1)

    def one_group(group, carry):
        source = lax.rem(start * chip_tiles + group * PERIOD_TILES, tiles)
        for which in range(PERIOD):
            first, offset = divmod(which * TLEN, LANES)
            pieces = []
            for part in range(DEPTH_TILES):
                begin = pl.multiple_of((source + first + part) * LANES, LANES)
                piece = raw_ref[:, pl.ds(begin, LANES)].astype(jnp.float32)
                if offset:
                    piece = pltpu.roll(piece, LANES - offset, 1)
                pieces.append(piece)
            row = pl.multiple_of((group * PERIOD + which) * SUBLANES, SUBLANES)
            for part in range(DEPTH_TILES):
                value = pieces[part]
                if part + 1 < DEPTH_TILES:
                    if offset:
                        value = jnp.where(lane < LANES - offset, value, pieces[part + 1])
                else:
                    value = jnp.where(lane < last, value, 0.0)
                rows[part, pl.ds(row, channels), :] = value
        return carry

    lax.fori_loop(0, groups, one_group, 0, unroll=8)

    station_row = lax.broadcasted_iota(jnp.int32, (stations, LANES), 0)
    avail = avail_ref[...].astype(jnp.float32)
    def per_row(by_station):
        return lax.dot_general(
            avail, by_station, (((0,), (0,)), ((), ())), preferred_element_type=jnp.float32
        )

    for factor_ref in factor_refs:
        usable_here = jnp.zeros((stations, LANES), jnp.float32)
        for station in range(stations):
            number = sum(usable_ref[station * COMPONENTS + part] for part in range(COMPONENTS))
            usable_here = jnp.where(station_row == station, number.astype(jnp.float32), usable_here)
        avail_cols[stations_here] = per_row(usable_here)
        counted = avail_cols[stations_here, pl.ds(pl.multiple_of(me * own, own), own), :]
        factor_ref[...] = math.sqrt(TLEN) * lax.rsqrt(jnp.maximum(counted, 1.0))
    for local_station in range(stations_here):
        chosen = station_row == me * stations_here + local_station
        avail_cols[local_station] = per_row(chosen.astype(jnp.float32))

    block_lane = lax.broadcasted_iota(jnp.int32, (own, LANES), 1)

    def one_channel(channel, carry):
        use = usable_ref[me * channels + channel].astype(jnp.float32)
        for place in range(2 * len(taken)):
            core, chip = divmod(place, len(taken))
            owner = me ^ (2 * taken[chip] + core)
            moved = lax.rem(owner // 2 - start + chips, chips) * chip_rows + owner % 2 * own
            here = pl.ds(moved * SUBLANES + channel, own, stride=SUBLANES)
            parts = [rows[part, here, :] for part in range(DEPTH_TILES)]
            mean = jnp.sum(sum(parts), axis=1, keepdims=True) * (1.0 / TLEN)
            centred = [value - mean for value in parts]
            centred[-1] = jnp.where(block_lane < last, centred[-1], 0.0)
            squared = jnp.sum(sum(value * value for value in centred), axis=1, keepdims=True)
            there = pl.ds(pl.multiple_of(owner * own, own), own)
            weight = avail_cols[channel // COMPONENTS, there, :] * use
            factor = lax.rsqrt(squared + EPSILON) * weight
            for part in range(DEPTH_TILES):
                out_ref[
                    channel, place * own : (place + 1) * own, part * LANES : (part + 1) * LANES
                ] = (centred[part] * factor).astype(jnp.bfloat16)
        return carry

    lax.fori_loop(0, channels, one_channel, 0, unroll=2)


def weighted_templates(raw, available, usable, token, shares, stay):
    channels, width = raw.shape
    stations, count = available.shape
    taken = 2 * count // shares if stay else count - 2 * count // shares
    outs = [jax.ShapeDtypeStruct((channels, taken, DEPTH), jnp.bfloat16)]
    if stay:
        outs.append(jax.ShapeDtypeStruct((count // shares, LANES), jnp.float32))
    return pl.pallas_call(
        functools.partial(template_kernel, shares, stay),
        out_shape=outs,
        in_specs=[
            pl.BlockSpec(memory_space=pltpu.VMEM),
            pl.BlockSpec(memory_space=pltpu.VMEM),
            pl.BlockSpec(memory_space=pltpu.SMEM),
            pl.BlockSpec(memory_space=pltpu.VMEM),
        ],
        out_specs=[pl.BlockSpec(memory_space=pltpu.VMEM)] * len(outs),
        scratch_shapes=[
            pltpu.VMEM((DEPTH_TILES, taken * SUBLANES, LANES), jnp.float32),
            pltpu.VMEM((channels // COMPONENTS + 1, count, LANES), jnp.float32),
        ],
        compiler_params=pltpu.CompilerParams(vmem_limit_bytes=VMEM_LIMIT),
        cost_estimate=pl.CostEstimate(flops=1 << 10, transcendentals=0, bytes_accessed=1 << 10),
        name="templates_staying" if stay else "templates_leaving",
    )(raw, available, usable, token)


def ahead(value, by):
    return pltpu.roll(value, value.shape[1] - by, 1) if by else value


def windows_kernel(blocks, *refs):
    segments = refs[:blocks]
    windows, scale, record, starts = refs[blocks:]
    channels, segment = segments[0].shape
    lags = blocks * segment
    wide = record.shape[1]
    base = windows.shape[2]
    me = lax.axis_index("blk")

    record[:, lags:] = jnp.zeros((SUBLANES, wide - lags), jnp.float32)
    for by in range(blocks):
        start = pl.multiple_of((me ^ by) * segment, LANES)
        record[0:channels, pl.ds(start, segment)] = segments[by][...].astype(jnp.float32)

    sums = {1: record[...] * record[...]}
    span = 1
    while 2 * span <= TLEN:
        sums[2 * span] = sums[span] + ahead(sums[span], span)
        span *= 2
    energy, taken = None, 0
    while taken < TLEN:
        if taken + span <= TLEN:
            term = sums[span][:, taken : taken + lags]
            energy = term if energy is None else energy + term
            taken += span
        span //= 2
    scale[...] = lax.rsqrt(jnp.maximum(energy, FLOOR_SHARE * TLEN))

    sublane = lax.broadcasted_iota(jnp.int32, (SUBLANES, wide), 0)
    for channel in range(channels):
        shifted = jnp.broadcast_to(record[channel : channel + 1, :], (SUBLANES, wide))
        for bit in (1, 2, 4):
            shifted = jnp.where((sublane & bit) != 0, ahead(shifted, bit), shifted)
        pair = jnp.concatenate([shifted, ahead(shifted, SUBLANES)], axis=0).astype(jnp.bfloat16)
        starts[channel] = pair
        windows[channel, : 2 * SUBLANES, :] = pair[:, :base]

    def one_channel(channel, carry):
        pair = starts[channel]
        for row in range(2 * SUBLANES, LANES, 2 * SUBLANES):
            windows[channel, row : row + 2 * SUBLANES, :] = pair[:, row : row + base]
        return carry

    lax.fori_loop(0, channels, one_channel, 0, unroll=3)


def all_windows(segments, name):
    channels, segment = segments[0].shape
    blocks = len(segments)
    lags = blocks * segment
    return pl.pallas_call(
        functools.partial(windows_kernel, blocks),
        out_shape=(
            jax.ShapeDtypeStruct((channels, LANES, lags + DEPTH - LANES), jnp.bfloat16),
            jax.ShapeDtypeStruct((SUBLANES, lags), jnp.float32),
        ),
        in_specs=[pl.BlockSpec(memory_space=pltpu.VMEM)] * blocks,
        out_specs=(pl.BlockSpec(memory_space=pltpu.VMEM),) * 2,
        scratch_shapes=[
            pltpu.VMEM((SUBLANES, lags + DEPTH), jnp.float32),
            pltpu.VMEM((channels, 2 * SUBLANES, lags + DEPTH), jnp.bfloat16),
        ],
        compiler_params=pltpu.CompilerParams(vmem_limit_bytes=VMEM_LIMIT),
        cost_estimate=pl.CostEstimate(flops=1 << 10, transcendentals=0, bytes_accessed=1 << 10),
        name=name,
    )(*segments)


def correlate_kernel(weighted_ref, windows, scale, *outs):
    channels, count, depth = weighted_ref.shape
    lags = scale.shape[1]
    rows = count // len(outs)
    tile = next(by for by in (16 * LANES, 8 * LANES, 4 * LANES, 2 * LANES) if lags % by == 0)

    def one_tile(first):
        here = pl.ds(first, tile)
        total = None
        for channel in range(channels):
            signal = jnp.concatenate(
                [
                    windows[
                        channel,
                        : min(LANES, TLEN - part * LANES),
                        pl.ds(pl.multiple_of(first + part * LANES, LANES), tile),
                    ]
                    for part in range(depth // LANES)
                ],
                axis=0,
            )
            weights = weighted_ref[channel, :, :TLEN]
            matched = jnp.dot(weights, signal, preferred_element_type=jnp.float32)
            term = matched * scale[channel : channel + 1, here]
            total = term if total is None else total + term
        for place, out in enumerate(outs):
            out[:, here] = total[place * rows : (place + 1) * rows].astype(out.dtype)

    if lags == tile:
        one_tile(0)
    else:

        def one_step(step, carry):
            one_tile(pl.multiple_of(step * tile, LANES))
            return carry

        lax.fori_loop(0, lags // tile, one_step, 0)


def correlations(weighted, windows, scale, blocks, name):
    channels, count, depth = weighted.shape
    lags = scale.shape[1]
    kinds = [jnp.float32] * (blocks // 2) + [jnp.bfloat16] * (blocks // 2)
    return pl.pallas_call(
        correlate_kernel,
        out_shape=[jax.ShapeDtypeStruct((count // blocks, lags), kind) for kind in kinds],
        in_specs=[pl.BlockSpec(memory_space=pltpu.VMEM)] * 3,
        out_specs=[pl.BlockSpec(memory_space=pltpu.VMEM)] * blocks,
        compiler_params=pltpu.CompilerParams(vmem_limit_bytes=VMEM_LIMIT),
        cost_estimate=pl.CostEstimate(flops=1 << 10, transcendentals=0, bytes_accessed=1 << 10),
        name=name,
    )(weighted, windows, scale)


def first_kernel(token_ref):
    token_ref[...] = jnp.zeros_like(token_ref)


def first():
    return pl.pallas_call(
        first_kernel,
        out_shape=jax.ShapeDtypeStruct((SUBLANES, LANES), jnp.float32),
        out_specs=pl.BlockSpec(memory_space=pltpu.VMEM),
        cost_estimate=pl.CostEstimate(flops=1 << 36, transcendentals=0, bytes_accessed=1 << 26),
        compiler_params=pltpu.CompilerParams(vmem_limit_bytes=1 << 20),
        name="first",
    )()


def add_kernel(*refs):
    total = refs[0][...]
    for ref in refs[1:-1]:
        total = total + ref[...].astype(jnp.float32)
    refs[-1][...] = total


def added(*terms):
    return pl.pallas_call(
        add_kernel,
        out_shape=jax.ShapeDtypeStruct(terms[0].shape, jnp.float32),
        in_specs=[pl.BlockSpec(memory_space=pltpu.VMEM)] * len(terms),
        out_specs=pl.BlockSpec(memory_space=pltpu.VMEM),
        cost_estimate=pl.CostEstimate(flops=1 << 36, transcendentals=0, bytes_accessed=1 << 26),
        compiler_params=pltpu.CompilerParams(vmem_limit_bytes=4 << 20),
        name="added",
    )(*terms)


def scale_kernel(factor_ref, *refs):
    factor = factor_ref[...]
    for start in range(0, refs[-1].shape[1], LANES):
        here = slice(start, start + LANES)
        total = refs[0][:, here]
        for ref in refs[1:-1]:
            total = total + ref[:, here].astype(jnp.float32)
        refs[-1][:, here] = total * factor


def scaled(factor, *terms):
    return pl.pallas_call(
        scale_kernel,
        out_shape=jax.ShapeDtypeStruct(terms[0].shape, jnp.float32),
        in_specs=[pl.BlockSpec(memory_space=pltpu.VMEM)] * (1 + len(terms)),
        out_specs=pl.BlockSpec(memory_space=pltpu.VMEM),
        compiler_params=pltpu.CompilerParams(vmem_limit_bytes=4 << 20),
        cost_estimate=pl.CostEstimate(flops=1 << 10, transcendentals=0, bytes_accessed=1 << 10),
        name="scaled",
    )(factor, *terms)


def local(waveforms, templates, available, usable):
    blocks = lax.axis_size("blk")
    shares = lax.axis_size("sta")
    chips = shares // 2

    waveforms, token = lax.optimization_barrier((waveforms, first()))
    segments = {0: waveforms}
    for by in range(1, blocks):
        segments[by] = exchanged(waveforms, "blk", by)
    segments = [segments[by] for by in range(blocks)]

    wide, narrow = jnp.float32, jnp.bfloat16
    (weighted,) = weighted_templates(templates, available, usable, token, shares, False)
    windows, scale = all_windows(segments, "windows")
    sums = correlations(weighted, windows, scale, 2 * (chips - 1), "correlate_leaving")
    order = sorted(range(1, chips), key=lambda by: (by != chips // 2, by))
    partner = {by: exchanged(sums[chips - 1 + by - 1], "sta", 1) for by in order}
    sent = []
    for by in order:
        own = sums[by - 1]
        if sent:
            own, sent[-1] = lax.optimization_barrier((own, sent[-1]))
        sent.append((own + partner[by].astype(wide)).astype(narrow))
    sent[-1], scale, later = lax.optimization_barrier((sent[-1], scale, token))
    arrived = [exchanged(term, "sta", 2 * by) for by, term in zip(order, sent)]

    weighted, factor = weighted_templates(templates, available, usable, later, shares, True)
    mine, other = correlations(weighted, windows, scale, 2, "correlate_staying")
    return scaled(factor, added(mine, *arrived), exchanged(other, "sta", 1))


def solution(mesh):
    return jax.shard_map(
        local,
        mesh=mesh,
        in_specs=(P("sta", "blk"), P("sta", "blk"), P(None, "blk"), P()),
        out_specs=P(("blk", "sta"), None),
        check_vma=False,
    )
```

```python
import functools
import math

import jax
import jax.numpy as jnp
from jax import lax
from jax.experimental import pallas as pl
from jax.experimental.pallas import tpu as pltpu
from jax.sharding import PartitionSpec as P

TLEN = 400
COMPONENTS = 3
LANES = 128
SUBLANES = 8

FLOOR_SHARE = 0.1
EPSILON = 1e-06

PERIOD = LANES // math.gcd(TLEN, LANES)
PERIOD_TILES = PERIOD * TLEN // LANES
DEPTH_TILES = -(-TLEN // LANES)
DEPTH = DEPTH_TILES * LANES
VMEM_LIMIT = 24 << 20


def exchanged(array, axis, by):
    length = lax.axis_size(axis)
    return lax.ppermute(array, axis, [(i, i ^ by) for i in range(length)])


def template_kernel(
    shares, stay, raw_ref, avail_ref, usable_ref, token_ref, *refs
):
    out_ref, *factor_refs, rows, avail_cols = refs
    channels, width = raw_ref.shape
    stations, count = avail_ref.shape
    tiles = width // LANES
    stations_here = channels // COMPONENTS
    own = count // shares
    chips = shares // 2
    chip_rows = 2 * own
    chip_tiles = tiles // chips
    taken = range(1) if stay else range(1, chips)
    groups = len(taken) * chip_rows // PERIOD
    me = lax.axis_index("sta")
    start = me // 2 if stay else me // 2 + 1
    last = TLEN - (DEPTH_TILES - 1) * LANES
    lane = lax.broadcasted_iota(jnp.int32, (channels, LANES), 1)

    def one_group(group, carry):
        source = lax.rem(start * chip_tiles + group * PERIOD_TILES, tiles)
        for which in range(PERIOD):
            first, offset = divmod(which * TLEN, LANES)
            pieces = []
            for part in range(DEPTH_TILES):
                begin = pl.multiple_of((source + first + part) * LANES, LANES)
                piece = raw_ref[:, pl.ds(begin, LANES)].astype(jnp.float32)
                if offset:
                    piece = pltpu.roll(piece, LANES - offset, 1)
                pieces.append(piece)
            row = pl.multiple_of((group * PERIOD + which) * SUBLANES, SUBLANES)
            for part in range(DEPTH_TILES):
                value = pieces[part]
                if part + 1 < DEPTH_TILES:
                    if offset:
                        value = jnp.where(lane < LANES - offset, value, pieces[part + 1])
                else:
                    value = jnp.where(lane < last, value, 0.0)
                rows[part, pl.ds(row, channels), :] = value
        return carry

    lax.fori_loop(0, groups, one_group, 0, unroll=8)

    station_row = lax.broadcasted_iota(jnp.int32, (stations, LANES), 0)
    avail = avail_ref[...].astype(jnp.float32)
    def per_row(by_station):
        return lax.dot_general(
            avail, by_station, (((0,), (0,)), ((), ())), preferred_element_type=jnp.float32
        )

    for factor_ref in factor_refs:
        usable_here = jnp.zeros((stations, LANES), jnp.float32)
        for station in range(stations):
            number = sum(usable_ref[station * COMPONENTS + part] for part in range(COMPONENTS))
            usable_here = jnp.where(station_row == station, number.astype(jnp.float32), usable_here)
        avail_cols[stations_here] = per_row(usable_here)
        counted = avail_cols[stations_here, pl.ds(pl.multiple_of(me * own, own), own), :]
        factor_ref[...] = math.sqrt(TLEN) * lax.rsqrt(jnp.maximum(counted, 1.0))
    for local_station in range(stations_here):
        chosen = station_row == me * stations_here + local_station
        avail_cols[local_station] = per_row(chosen.astype(jnp.float32))

    block_lane = lax.broadcasted_iota(jnp.int32, (own, LANES), 1)

    def one_channel(channel, carry):
        use = usable_ref[me * channels + channel].astype(jnp.float32)
        for place in range(2 * len(taken)):
            core, chip = divmod(place, len(taken))
            owner = me ^ (2 * taken[chip] + core)
            moved = lax.rem(owner // 2 - start + chips, chips) * chip_rows + owner % 2 * own
            here = pl.ds(moved * SUBLANES + channel, own, stride=SUBLANES)
            parts = [rows[part, here, :] for part in range(DEPTH_TILES)]
            mean = jnp.sum(sum(parts), axis=1, keepdims=True) * (1.0 / TLEN)
            centred = [value - mean for value in parts]
            centred[-1] = jnp.where(block_lane < last, centred[-1], 0.0)
            squared = jnp.sum(sum(value * value for value in centred), axis=1, keepdims=True)
            there = pl.ds(pl.multiple_of(owner * own, own), own)
            weight = avail_cols[channel // COMPONENTS, there, :] * use
            factor = lax.rsqrt(squared + EPSILON) * weight
            for part in range(DEPTH_TILES):
                out_ref[
                    channel, place * own : (place + 1) * own, part * LANES : (part + 1) * LANES
                ] = (centred[part] * factor).astype(jnp.bfloat16)
        return carry

    lax.fori_loop(0, channels, one_channel, 0, unroll=2)


def weighted_templates(raw, available, usable, token, shares, stay):
    channels, width = raw.shape
    stations, count = available.shape
    taken = 2 * count // shares if stay else count - 2 * count // shares
    outs = [jax.ShapeDtypeStruct((channels, taken, DEPTH), jnp.bfloat16)]
    if stay:
        outs.append(jax.ShapeDtypeStruct((count // shares, LANES), jnp.float32))
    return pl.pallas_call(
        functools.partial(template_kernel, shares, stay),
        out_shape=outs,
        in_specs=[
            pl.BlockSpec(memory_space=pltpu.VMEM),
            pl.BlockSpec(memory_space=pltpu.VMEM),
            pl.BlockSpec(memory_space=pltpu.SMEM),
            pl.BlockSpec(memory_space=pltpu.VMEM),
        ],
        out_specs=[pl.BlockSpec(memory_space=pltpu.VMEM)] * len(outs),
        scratch_shapes=[
            pltpu.VMEM((DEPTH_TILES, (taken + 1) * SUBLANES, LANES), jnp.float32),
            pltpu.VMEM((channels // COMPONENTS + 1, count, LANES), jnp.float32),
        ],
        compiler_params=pltpu.CompilerParams(vmem_limit_bytes=VMEM_LIMIT),
        cost_estimate=pl.CostEstimate(flops=1 << 10, transcendentals=0, bytes_accessed=1 << 10),
        name="templates_staying" if stay else "templates_leaving",
    )(raw, available, usable, token)


def ahead(value, by):
    return pltpu.roll(value, value.shape[1] - by, 1) if by else value


def windows_kernel(blocks, *refs):
    segments = refs[:blocks]
    windows, scale, record, starts = refs[blocks:]
    channels, segment = segments[0].shape
    lags = blocks * segment
    wide = record.shape[1]
    base = windows.shape[2]
    me = lax.axis_index("blk")

    record[:, lags:] = jnp.zeros((SUBLANES, wide - lags), jnp.float32)
    for by in range(blocks):
        start = pl.multiple_of((me ^ by) * segment, LANES)
        record[0:channels, pl.ds(start, segment)] = segments[by][...].astype(jnp.float32)

    sums = {1: record[...] * record[...]}
    span = 1
    while 2 * span <= TLEN:
        sums[2 * span] = sums[span] + ahead(sums[span], span)
        span *= 2
    energy, taken = None, 0
    while taken < TLEN:
        if taken + span <= TLEN:
            term = sums[span][:, taken : taken + lags]
            energy = term if energy is None else energy + term
            taken += span
        span //= 2
    scale[...] = lax.rsqrt(jnp.maximum(energy, FLOOR_SHARE * TLEN))

    sublane = lax.broadcasted_iota(jnp.int32, (SUBLANES, wide), 0)
    for channel in range(channels):
        shifted = jnp.broadcast_to(record[channel : channel + 1, :], (SUBLANES, wide))
        for bit in (1, 2, 4):
            shifted = jnp.where((sublane & bit) != 0, ahead(shifted, bit), shifted)
        pair = jnp.concatenate([shifted, ahead(shifted, SUBLANES)], axis=0).astype(jnp.bfloat16)
        starts[channel] = pair
        windows[channel, : 2 * SUBLANES, :] = pair[:, :base]

    def one_channel(channel, carry):
        pair = starts[channel]
        for row in range(2 * SUBLANES, LANES, 2 * SUBLANES):
            windows[channel, row : row + 2 * SUBLANES, :] = pair[:, row : row + base]
        return carry

    lax.fori_loop(0, channels, one_channel, 0, unroll=3)


def all_windows(segments, name):
    channels, segment = segments[0].shape
    blocks = len(segments)
    lags = blocks * segment
    return pl.pallas_call(
        functools.partial(windows_kernel, blocks),
        out_shape=(
            jax.ShapeDtypeStruct((channels, LANES, lags + DEPTH - LANES), jnp.bfloat16),
            jax.ShapeDtypeStruct((SUBLANES, lags), jnp.float32),
        ),
        in_specs=[pl.BlockSpec(memory_space=pltpu.VMEM)] * blocks,
        out_specs=(pl.BlockSpec(memory_space=pltpu.VMEM),) * 2,
        scratch_shapes=[
            pltpu.VMEM((SUBLANES, lags + DEPTH), jnp.float32),
            pltpu.VMEM((channels, 2 * SUBLANES, lags + DEPTH), jnp.bfloat16),
        ],
        compiler_params=pltpu.CompilerParams(vmem_limit_bytes=VMEM_LIMIT),
        cost_estimate=pl.CostEstimate(flops=1 << 10, transcendentals=0, bytes_accessed=1 << 10),
        name=name,
    )(*segments)


def correlate_kernel(weighted_ref, windows, scale, *outs):
    channels, count, depth = weighted_ref.shape
    lags = scale.shape[1]
    rows = count // len(outs)
    tile = next(by for by in (16 * LANES, 8 * LANES, 4 * LANES, 2 * LANES) if lags % by == 0)

    def one_tile(first):
        here = pl.ds(first, tile)
        total = None
        for channel in range(channels):
            signal = jnp.concatenate(
                [
                    windows[
                        channel,
                        : min(LANES, TLEN - part * LANES),
                        pl.ds(pl.multiple_of(first + part * LANES, LANES), tile),
                    ]
                    for part in range(depth // LANES)
                ],
                axis=0,
            )
            weights = weighted_ref[channel, :, :TLEN]
            matched = jnp.dot(weights, signal, preferred_element_type=jnp.float32)
            term = matched * scale[channel : channel + 1, here]
            total = term if total is None else total + term
        for place, out in enumerate(outs):
            out[:, here] = total[place * rows : (place + 1) * rows].astype(out.dtype)

    if lags == tile:
        one_tile(0)
    else:

        def one_step(step, carry):
            one_tile(pl.multiple_of(step * tile, LANES))
            return carry

        lax.fori_loop(0, lags // tile, one_step, 0)


def correlations(weighted, windows, scale, blocks, name):
    channels, count, depth = weighted.shape
    lags = scale.shape[1]
    kinds = [jnp.float32] * (blocks // 2) + [jnp.bfloat16] * (blocks // 2)
    return pl.pallas_call(
        correlate_kernel,
        out_shape=[jax.ShapeDtypeStruct((count // blocks, lags), kind) for kind in kinds],
        in_specs=[pl.BlockSpec(memory_space=pltpu.VMEM)] * 3,
        out_specs=[pl.BlockSpec(memory_space=pltpu.VMEM)] * blocks,
        compiler_params=pltpu.CompilerParams(vmem_limit_bytes=VMEM_LIMIT),
        cost_estimate=pl.CostEstimate(flops=1 << 10, transcendentals=0, bytes_accessed=1 << 10),
        name=name,
    )(weighted, windows, scale)


def first_kernel(token_ref):
    token_ref[...] = jnp.zeros_like(token_ref)


def first():
    return pl.pallas_call(
        first_kernel,
        out_shape=jax.ShapeDtypeStruct((SUBLANES, LANES), jnp.float32),
        out_specs=pl.BlockSpec(memory_space=pltpu.VMEM),
        cost_estimate=pl.CostEstimate(flops=1 << 36, transcendentals=0, bytes_accessed=1 << 26),
        compiler_params=pltpu.CompilerParams(vmem_limit_bytes=1 << 20),
        name="first",
    )()


def add_kernel(*refs):
    total = refs[0][...]
    for ref in refs[1:-1]:
        total = total + ref[...].astype(jnp.float32)
    refs[-1][...] = total


def added(*terms):
    return pl.pallas_call(
        add_kernel,
        out_shape=jax.ShapeDtypeStruct(terms[0].shape, jnp.float32),
        in_specs=[pl.BlockSpec(memory_space=pltpu.VMEM)] * len(terms),
        out_specs=pl.BlockSpec(memory_space=pltpu.VMEM),
        cost_estimate=pl.CostEstimate(flops=1 << 36, transcendentals=0, bytes_accessed=1 << 26),
        compiler_params=pltpu.CompilerParams(vmem_limit_bytes=4 << 20),
        name="added",
    )(*terms)


def scale_kernel(factor_ref, *refs):
    factor = factor_ref[...]
    for start in range(0, refs[-1].shape[1], LANES):
        here = slice(start, start + LANES)
        total = refs[0][:, here]
        for ref in refs[1:-1]:
            total = total + ref[:, here].astype(jnp.float32)
        refs[-1][:, here] = total * factor


def scaled(factor, *terms):
    return pl.pallas_call(
        scale_kernel,
        out_shape=jax.ShapeDtypeStruct(terms[0].shape, jnp.float32),
        in_specs=[pl.BlockSpec(memory_space=pltpu.VMEM)] * (1 + len(terms)),
        out_specs=pl.BlockSpec(memory_space=pltpu.VMEM),
        compiler_params=pltpu.CompilerParams(vmem_limit_bytes=4 << 20),
        cost_estimate=pl.CostEstimate(flops=1 << 10, transcendentals=0, bytes_accessed=1 << 10),
        name="scaled",
    )(factor, *terms)


def local(waveforms, templates, available, usable):
    blocks = lax.axis_size("blk")
    shares = lax.axis_size("sta")
    chips = shares // 2

    waveforms, token = lax.optimization_barrier((waveforms, first()))
    segments = {0: waveforms}
    for by in range(1, blocks):
        segments[by] = exchanged(waveforms, "blk", by)
    segments = [segments[by] for by in range(blocks)]

    wide, narrow = jnp.float32, jnp.bfloat16
    (weighted,) = weighted_templates(templates, available, usable, token, shares, False)
    windows, scale = all_windows(segments, "windows")
    sums = correlations(weighted, windows, scale, 2 * (chips - 1), "correlate_leaving")
    order = sorted(range(1, chips), key=lambda by: (by != chips // 2, by))
    partner = {by: exchanged(sums[chips - 1 + by - 1], "sta", 1) for by in order}
    sent = []
    for by in order:
        own = sums[by - 1]
        if sent:
            own, sent[-1] = lax.optimization_barrier((own, sent[-1]))
        sent.append((own + partner[by].astype(wide)).astype(narrow))
    sent[-1], scale, later = lax.optimization_barrier((sent[-1], scale, token))
    arrived = [exchanged(term, "sta", 2 * by) for by, term in zip(order, sent)]

    weighted, factor = weighted_templates(templates, available, usable, later, shares, True)
    mine, other = correlations(weighted, windows, scale, 2, "correlate_staying")
    return scaled(factor, added(mine, *arrived), exchanged(other, "sta", 1))


def solution(mesh):
    return jax.shard_map(
        local,
        mesh=mesh,
        in_specs=(P("sta", "blk"), P("sta", "blk"), P(None, "blk"), P()),
        out_specs=P(("blk", "sta"), None),
        check_vma=False,
    )
```

```python
import functools
import math

import jax
import jax.numpy as jnp
from jax import lax
from jax.experimental import pallas as pl
from jax.experimental.pallas import tpu as pltpu
from jax.sharding import PartitionSpec as P

TLEN = 400
COMPONENTS = 3
LANES = 128
SUBLANES = 8

FLOOR_SHARE = 0.1
EPSILON = 1e-06

PERIOD = LANES // math.gcd(TLEN, LANES)
PERIOD_TILES = PERIOD * TLEN // LANES
DEPTH_TILES = -(-TLEN // LANES)
DEPTH = DEPTH_TILES * LANES
VMEM_LIMIT = 24 << 20


def exchanged(array, axis, by):
    length = lax.axis_size(axis)
    return lax.ppermute(array, axis, [(i, i ^ by) for i in range(length)])


def template_kernel(
    shares, stay, raw_ref, avail_ref, usable_ref, token_ref, *refs
):
    out_ref, *factor_refs, rows, avail_cols = refs
    channels, width = raw_ref.shape
    stations, count = avail_ref.shape
    tiles = width // LANES
    stations_here = channels // COMPONENTS
    own = count // shares
    chips = shares // 2
    chip_rows = 2 * own
    chip_tiles = tiles // chips
    taken = range(1) if stay else range(1, chips)
    groups = len(taken) * chip_rows // PERIOD
    me = lax.axis_index("sta")
    start = me // 2 if stay else me // 2 + 1
    last = TLEN - (DEPTH_TILES - 1) * LANES
    lane = lax.broadcasted_iota(jnp.int32, (channels, LANES), 1)

    def one_group(group, carry):
        source = lax.rem(start * chip_tiles + group * PERIOD_TILES, tiles)
        for which in range(PERIOD):
            first, offset = divmod(which * TLEN, LANES)
            pieces = []
            for part in range(DEPTH_TILES):
                begin = pl.multiple_of((source + first + part) * LANES, LANES)
                piece = raw_ref[:, pl.ds(begin, LANES)].astype(jnp.float32)
                if offset:
                    piece = pltpu.roll(piece, LANES - offset, 1)
                pieces.append(piece)
            row = pl.multiple_of((group * PERIOD + which) * SUBLANES, SUBLANES)
            for part in range(DEPTH_TILES):
                value = pieces[part]
                if part + 1 < DEPTH_TILES:
                    if offset:
                        value = jnp.where(lane < LANES - offset, value, pieces[part + 1])
                else:
                    value = jnp.where(lane < last, value, 0.0)
                rows[part, pl.ds(row, channels), :] = value
        return carry

    lax.fori_loop(0, groups, one_group, 0, unroll=8)

    station_row = lax.broadcasted_iota(jnp.int32, (stations, LANES), 0)
    avail = avail_ref[...].astype(jnp.float32)
    def per_row(by_station):
        return lax.dot_general(
            avail, by_station, (((0,), (0,)), ((), ())), preferred_element_type=jnp.float32
        )

    for factor_ref in factor_refs:
        usable_here = jnp.zeros((stations, LANES), jnp.float32)
        for station in range(stations):
            number = sum(usable_ref[station * COMPONENTS + part] for part in range(COMPONENTS))
            usable_here = jnp.where(station_row == station, number.astype(jnp.float32), usable_here)
        avail_cols[stations_here] = per_row(usable_here)
        counted = avail_cols[stations_here, pl.ds(pl.multiple_of(me * own, own), own), :]
        factor_ref[...] = math.sqrt(TLEN) * lax.rsqrt(jnp.maximum(counted, 1.0))
    for local_station in range(stations_here):
        chosen = station_row == me * stations_here + local_station
        avail_cols[local_station] = per_row(chosen.astype(jnp.float32))

    block_lane = lax.broadcasted_iota(jnp.int32, (own, LANES), 1)

    def one_channel(channel, carry):
        use = usable_ref[me * channels + channel].astype(jnp.float32)
        for place in range(2 * len(taken)):
            core, chip = divmod(place, len(taken))
            owner = me ^ (2 * taken[chip] + core)
            moved = lax.rem(owner // 2 - start + chips, chips) * chip_rows + owner % 2 * own
            here = pl.ds(moved * SUBLANES + channel, own, stride=SUBLANES)
            parts = [rows[part, here, :] for part in range(DEPTH_TILES)]
            mean = jnp.sum(sum(parts), axis=1, keepdims=True) * (1.0 / TLEN)
            centred = [value - mean for value in parts]
            centred[-1] = jnp.where(block_lane < last, centred[-1], 0.0)
            squared = jnp.sum(sum(value * value for value in centred), axis=1, keepdims=True)
            there = pl.ds(pl.multiple_of(owner * own, own), own)
            weight = avail_cols[channel // COMPONENTS, there, :] * use
            factor = lax.rsqrt(squared + EPSILON) * weight
            for part in range(DEPTH_TILES):
                out_ref[
                    channel, place * own : (place + 1) * own, part * LANES : (part + 1) * LANES
                ] = (centred[part] * factor).astype(jnp.bfloat16)
        return carry

    lax.fori_loop(0, channels, one_channel, 0, unroll=2)


def weighted_templates(raw, available, usable, token, shares, stay):
    channels, width = raw.shape
    stations, count = available.shape
    taken = 2 * count // shares if stay else count - 2 * count // shares
    outs = [jax.ShapeDtypeStruct((channels, taken, DEPTH), jnp.bfloat16)]
    if stay:
        outs.append(jax.ShapeDtypeStruct((count // shares, LANES), jnp.float32))
    return pl.pallas_call(
        functools.partial(template_kernel, shares, stay),
        out_shape=outs,
        in_specs=[
            pl.BlockSpec(memory_space=pltpu.VMEM),
            pl.BlockSpec(memory_space=pltpu.VMEM),
            pl.BlockSpec(memory_space=pltpu.SMEM),
            pl.BlockSpec(memory_space=pltpu.VMEM),
        ],
        out_specs=[pl.BlockSpec(memory_space=pltpu.VMEM)] * len(outs),
        scratch_shapes=[
            pltpu.VMEM((DEPTH_TILES, (taken + 1) * SUBLANES, LANES), jnp.float32),
            pltpu.VMEM((channels // COMPONENTS + 1, count, LANES), jnp.float32),
        ],
        compiler_params=pltpu.CompilerParams(vmem_limit_bytes=VMEM_LIMIT),
        cost_estimate=pl.CostEstimate(flops=1 << 10, transcendentals=0, bytes_accessed=1 << 10),
        name="templates_staying" if stay else "templates_leaving",
    )(raw, available, usable, token)


def ahead(value, by):
    return pltpu.roll(value, value.shape[1] - by, 1) if by else value


def windows_kernel(blocks, *refs):
    segments = refs[:blocks]
    windows, scale, record, starts = refs[blocks:]
    channels, segment = segments[0].shape
    lags = blocks * segment
    wide = record.shape[1]
    base = windows.shape[2]
    me = lax.axis_index("blk")

    record[:, lags:] = jnp.zeros((SUBLANES, wide - lags), jnp.float32)
    for by in range(blocks):
        start = pl.multiple_of((me ^ by) * segment, LANES)
        record[0:channels, pl.ds(start, segment)] = segments[by][...].astype(jnp.float32)

    sums = {1: record[...] * record[...]}
    span = 1
    while 2 * span <= TLEN:
        sums[2 * span] = sums[span] + ahead(sums[span], span)
        span *= 2
    energy, taken = None, 0
    while taken < TLEN:
        if taken + span <= TLEN:
            term = sums[span][:, taken : taken + lags]
            energy = term if energy is None else energy + term
            taken += span
        span //= 2
    scale[...] = lax.rsqrt(jnp.maximum(energy, FLOOR_SHARE * TLEN))

    sublane = lax.broadcasted_iota(jnp.int32, (SUBLANES, wide), 0)
    for channel in range(channels):
        shifted = jnp.broadcast_to(record[channel : channel + 1, :], (SUBLANES, wide))
        for bit in (1, 2, 4):
            shifted = jnp.where((sublane & bit) != 0, ahead(shifted, bit), shifted)
        pair = jnp.concatenate([shifted, ahead(shifted, SUBLANES)], axis=0).astype(jnp.bfloat16)
        starts[channel] = pair
        windows[channel, : 2 * SUBLANES, :] = pair[:, :base]

    def one_channel(channel, carry):
        pair = starts[channel]
        for row in range(2 * SUBLANES, LANES, 2 * SUBLANES):
            windows[channel, row : row + 2 * SUBLANES, :] = pair[:, row : row + base]
        return carry

    lax.fori_loop(0, channels, one_channel, 0, unroll=6)


def all_windows(segments, name):
    channels, segment = segments[0].shape
    blocks = len(segments)
    lags = blocks * segment
    return pl.pallas_call(
        functools.partial(windows_kernel, blocks),
        out_shape=(
            jax.ShapeDtypeStruct((channels, LANES, lags + DEPTH - LANES), jnp.bfloat16),
            jax.ShapeDtypeStruct((SUBLANES, lags), jnp.float32),
        ),
        in_specs=[pl.BlockSpec(memory_space=pltpu.VMEM)] * blocks,
        out_specs=(pl.BlockSpec(memory_space=pltpu.VMEM),) * 2,
        scratch_shapes=[
            pltpu.VMEM((SUBLANES, lags + DEPTH), jnp.float32),
            pltpu.VMEM((channels, 2 * SUBLANES, lags + DEPTH), jnp.bfloat16),
        ],
        compiler_params=pltpu.CompilerParams(vmem_limit_bytes=VMEM_LIMIT),
        cost_estimate=pl.CostEstimate(flops=1 << 10, transcendentals=0, bytes_accessed=1 << 10),
        name=name,
    )(*segments)


def correlate_kernel(weighted_ref, windows, scale, *outs):
    channels, count, depth = weighted_ref.shape
    lags = scale.shape[1]
    rows = count // len(outs)
    tile = next(by for by in (16 * LANES, 8 * LANES, 4 * LANES, 2 * LANES) if lags % by == 0)

    def one_tile(first):
        here = pl.ds(first, tile)
        total = None
        for channel in range(channels):
            signal = jnp.concatenate(
                [
                    windows[
                        channel,
                        : min(LANES, TLEN - part * LANES),
                        pl.ds(pl.multiple_of(first + part * LANES, LANES), tile),
                    ]
                    for part in range(depth // LANES)
                ],
                axis=0,
            )
            weights = weighted_ref[channel, :, :TLEN]
            matched = jnp.dot(weights, signal, preferred_element_type=jnp.float32)
            term = matched * scale[channel : channel + 1, here]
            total = term if total is None else total + term
        for place, out in enumerate(outs):
            out[:, here] = total[place * rows : (place + 1) * rows].astype(out.dtype)

    if lags == tile:
        one_tile(0)
    else:

        def one_step(step, carry):
            one_tile(pl.multiple_of(step * tile, LANES))
            return carry

        lax.fori_loop(0, lags // tile, one_step, 0)


def correlations(weighted, windows, scale, blocks, name):
    channels, count, depth = weighted.shape
    lags = scale.shape[1]
    kinds = [jnp.float32] * (blocks // 2) + [jnp.bfloat16] * (blocks // 2)
    return pl.pallas_call(
        correlate_kernel,
        out_shape=[jax.ShapeDtypeStruct((count // blocks, lags), kind) for kind in kinds],
        in_specs=[pl.BlockSpec(memory_space=pltpu.VMEM)] * 3,
        out_specs=[pl.BlockSpec(memory_space=pltpu.VMEM)] * blocks,
        compiler_params=pltpu.CompilerParams(vmem_limit_bytes=VMEM_LIMIT),
        cost_estimate=pl.CostEstimate(flops=1 << 10, transcendentals=0, bytes_accessed=1 << 10),
        name=name,
    )(weighted, windows, scale)


def first_kernel(token_ref):
    token_ref[...] = jnp.zeros_like(token_ref)


def first():
    return pl.pallas_call(
        first_kernel,
        out_shape=jax.ShapeDtypeStruct((SUBLANES, LANES), jnp.float32),
        out_specs=pl.BlockSpec(memory_space=pltpu.VMEM),
        cost_estimate=pl.CostEstimate(flops=1 << 36, transcendentals=0, bytes_accessed=1 << 26),
        compiler_params=pltpu.CompilerParams(vmem_limit_bytes=1 << 20),
        name="first",
    )()


def add_kernel(*refs):
    total = refs[0][...]
    for ref in refs[1:-1]:
        total = total + ref[...].astype(jnp.float32)
    refs[-1][...] = total


def added(*terms):
    return pl.pallas_call(
        add_kernel,
        out_shape=jax.ShapeDtypeStruct(terms[0].shape, jnp.float32),
        in_specs=[pl.BlockSpec(memory_space=pltpu.VMEM)] * len(terms),
        out_specs=pl.BlockSpec(memory_space=pltpu.VMEM),
        cost_estimate=pl.CostEstimate(flops=1 << 36, transcendentals=0, bytes_accessed=1 << 26),
        compiler_params=pltpu.CompilerParams(vmem_limit_bytes=4 << 20),
        name="added",
    )(*terms)


def scale_kernel(factor_ref, *refs):
    factor = factor_ref[...]
    for start in range(0, refs[-1].shape[1], LANES):
        here = slice(start, start + LANES)
        total = refs[0][:, here]
        for ref in refs[1:-1]:
            total = total + ref[:, here].astype(jnp.float32)
        refs[-1][:, here] = total * factor


def scaled(factor, *terms):
    return pl.pallas_call(
        scale_kernel,
        out_shape=jax.ShapeDtypeStruct(terms[0].shape, jnp.float32),
        in_specs=[pl.BlockSpec(memory_space=pltpu.VMEM)] * (1 + len(terms)),
        out_specs=pl.BlockSpec(memory_space=pltpu.VMEM),
        compiler_params=pltpu.CompilerParams(vmem_limit_bytes=4 << 20),
        cost_estimate=pl.CostEstimate(flops=1 << 10, transcendentals=0, bytes_accessed=1 << 10),
        name="scaled",
    )(factor, *terms)


def local(waveforms, templates, available, usable):
    blocks = lax.axis_size("blk")
    shares = lax.axis_size("sta")
    chips = shares // 2

    waveforms, token = lax.optimization_barrier((waveforms, first()))
    segments = {0: waveforms}
    for by in range(1, blocks):
        segments[by] = exchanged(waveforms, "blk", by)
    segments = [segments[by] for by in range(blocks)]

    wide, narrow = jnp.float32, jnp.bfloat16
    (weighted,) = weighted_templates(templates, available, usable, token, shares, False)
    windows, scale = all_windows(segments, "windows")
    sums = correlations(weighted, windows, scale, 2 * (chips - 1), "correlate_leaving")
    order = sorted(range(1, chips), key=lambda by: (by != chips // 2, by))
    partner = {by: exchanged(sums[chips - 1 + by - 1], "sta", 1) for by in order}
    sent = []
    for by in order:
        own = sums[by - 1]
        if sent:
            own, sent[-1] = lax.optimization_barrier((own, sent[-1]))
        sent.append((own + partner[by].astype(wide)).astype(narrow))
    sent[-1], scale, later = lax.optimization_barrier((sent[-1], scale, token))
    arrived = [exchanged(term, "sta", 2 * by) for by, term in zip(order, sent)]

    weighted, factor = weighted_templates(templates, available, usable, later, shares, True)
    mine, other = correlations(weighted, windows, scale, 2, "correlate_staying")
    return scaled(factor, added(mine, *arrived), exchanged(other, "sta", 1))


def solution(mesh):
    return jax.shard_map(
        local,
        mesh=mesh,
        in_specs=(P("sta", "blk"), P("sta", "blk"), P(None, "blk"), P()),
        out_specs=P(("blk", "sta"), None),
        check_vma=False,
    )
```
